128 devices in a mesh: tok: 16 (over x, y), head: 8 (over z, core).
Axes of the slice: x: 4, y: 4, z: 4, core: 2. Of those that a mesh axis runs over, the one named last changes fastest.
Arguments:
- hidden: float32 [8192, 5376], P('tok', 'head'), may hold values from -8 to 8
- queries: float32 [8192, 2048], P('tok', 'head'), may hold values from -4000 to 4000
- out_grad: float32 [8192, 2048], P('tok', 'head'), may hold values from -6 to 6
- w_key: float32 [5376, 1024], P('head', 'tok'), may hold values from -1 to 1
- w_value: float32 [5376, 1024], P('head', 'tok'), may hold values from -0.078125 to 0.078125
- fork_tile: int32 [15], replicated, may hold values from 0 to 57, as said below
- live_len: int32 [16], replicated, may hold values from 257 to 512, as said below
Outputs:
- grad_query: float32 [8192, 2048], P('tok', 'head')
- grad_key: float32 [8192, 1024], P('tok', 'head')
- grad_value: float32 [8192, 1024], P('tok', 'head')
- grad_w_key: float32 [5376, 1024], P('head', 'tok')
- grad_w_value: float32 [5376, 1024], P('head', 'tok')
The draws below stay inside these ranges and needn't reach their ends.
Inputs may be any that keep to these rules, and one draw needn't show every extreme that they name: fork_tile[b - 1] lies in branch b - 1 or b - 2 (branch 0 counts), among that branch's first 2 tiles, and those tiles are live. `live_len`: branch 0 is fully live.
All inputs are finite; a program needn't handle non-finite values.
Results may differ from the reference program's by a relative error of at most 0.0005.
Values sent between devices are 32-bit elements; how exact they have to be, the bound alone decides.
A program may use at most 128 MiB of HBM per device.

```python
import jax
import jax.numpy as jnp
from jax import lax

D = 5376
HEADS = 16
KV_HEADS = 8
HEAD_DIM = 128
TILE = 128
CAP = 2
TOK_DEV = 512
TOKENS = 8192
N_TOK = 16


def draw_hidden(key, part):
    return jax.random.normal(jax.random.fold_in(key, 101), (TOKENS, D), jnp.float32)


def draw_w_key(key, part):
    return jax.random.normal(jax.random.fold_in(key, 102), (D, KV_HEADS * HEAD_DIM), jnp.float32) * D ** (-0.5)


def draw_queries(key, part):
    normal_rows = jax.random.normal(jax.random.fold_in(key, 103), (TOKENS, HEADS * HEAD_DIM), jnp.float32)
    return normal_rows


def draw_fork_tile(key, part):
    branches = TOKENS // TOK_DEV
    branch_ids = jnp.arange(1, branches)
    far_pick = jax.random.randint(jax.random.fold_in(key, 105), (branches - 1,), 0, 8)
    step_back = jnp.where(far_pick == 0, 2, 1)
    parent = jnp.maximum(branch_ids - step_back, 0)
    early_pick = jax.random.randint(jax.random.fold_in(key, 106), (branches - 1,), 0, 4)
    within = jnp.where(early_pick == 0, 0, CAP - 1)
    within = within.at[0].set(0)
    parent = parent.at[-1].set(branches - 2)
    within = within.at[-1].set(CAP - 1)
    return (parent * (TOK_DEV // TILE) + within).astype(jnp.int32)


def draw_live_len(key, part):
    branches = TOKENS // TOK_DEV
    lengths = jax.random.randint(jax.random.fold_in(key, 104), (branches,), TOK_DEV // 2 + 1, TOK_DEV + 1)
    lengths = lengths.at[0].set(TOK_DEV)
    lengths = lengths.at[1].set(TOK_DEV // 2 + 1)
    return lengths.astype(jnp.int32)


def level_of(rng, dims, shards, smallest, high):
    loudness, own = 1.0, jax.random.fold_in(rng, 6)
    for position, parts in shards:
        heights = jnp.exp(jax.random.uniform(jax.random.fold_in(own, position), (parts,), jnp.float32, smallest / len(shards), high / len(shards)))
        loudness = loudness * jnp.repeat(heights, dims[position] // parts).reshape([-1 if axis == position else 1 for axis in range(len(dims))])
    return loudness


def centred(key, dims, deviation, bound, cuts=(), kind=jnp.bfloat16):
    level = level_of(key, dims, cuts, -0.22, 0.18) if cuts else 1.0
    drawn = jax.random.normal(key, dims, jnp.float32) * deviation * level
    return jnp.minimum(jnp.maximum(drawn, -bound), bound).astype(kind)


def setup_inputs(seed: int = 0) -> dict:
    key_list = jax.random.split(jax.random.key(seed), 8)
    hidden = draw_hidden(jax.random.fold_in(key_list[7], 71), 0)
    queries = draw_queries(jax.random.fold_in(key_list[7], 71), 0)
    out_grad = centred(key_list[2], (TOKENS, HEADS * HEAD_DIM), 1.0, 6.0, ((0, 16), (1, 8)), jnp.float32)
    w_key = draw_w_key(jax.random.fold_in(key_list[7], 71), 0)
    w_value = centred(key_list[4], (D, KV_HEADS * HEAD_DIM), D ** -0.5, 0.078125, ((0, 8), (1, 16)), jnp.float32)
    fork_tile = draw_fork_tile(jax.random.fold_in(key_list[7], 71), 0)
    live_len = draw_live_len(jax.random.fold_in(key_list[7], 71), 0)
    return {"hidden": hidden, "queries": queries, "out_grad": out_grad, "w_key": w_key, "w_value": w_value, "fork_tile": fork_tile, "live_len": live_len}


logit_scale = 168.0 ** -0.5
highest = lax.Precision.HIGHEST


def path_table(fork_tile, owners, tile_count):
    initial = jnp.full((owners, owners), -1, jnp.int32)

    def visit_branch(branch, path_rows):
        fork_at = fork_tile[branch - 1]
        parent = fork_at // tile_count
        inherited = path_rows[parent].at[parent].set((fork_at % tile_count).astype(jnp.int32))
        return path_rows.at[branch].set(inherited)

    return lax.fori_loop(1, owners, visit_branch, initial)


def visible_mask(entries_row, live_count, row_count, owners):
    slot_index = jnp.arange(owners * CAP * TILE)
    owner_of = slot_index // (CAP * TILE)
    tile_of = (slot_index % (CAP * TILE)) // TILE
    remote = (tile_of <= entries_row[owner_of])[None, :]
    positions = jnp.arange(row_count)
    local_part = (positions[None, :] <= positions[:, None]) & (positions[None, :] < live_count)
    return jnp.concatenate([jnp.broadcast_to(remote, (row_count, remote.shape[1])), local_part], axis=1)


def attend(query_rows, grad_rows, key_rows, value_rows, visible):
    query_heads = query_rows.shape[1] // HEAD_DIM
    kv_heads = key_rows.shape[1] // HEAD_DIM
    group_size = query_heads // kv_heads
    query_grads = []
    key_grads = [jnp.zeros((key_rows.shape[0], HEAD_DIM), jnp.float32) for _ in range(kv_heads)]
    value_grads = [jnp.zeros((key_rows.shape[0], HEAD_DIM), jnp.float32) for _ in range(kv_heads)]
    for head_index in range(query_heads):
        kv_index = head_index // group_size
        query_head = query_rows[:, head_index * HEAD_DIM:(head_index + 1) * HEAD_DIM]
        grad_head = grad_rows[:, head_index * HEAD_DIM:(head_index + 1) * HEAD_DIM]
        key_head = key_rows[:, kv_index * HEAD_DIM:(kv_index + 1) * HEAD_DIM]
        value_head = value_rows[:, kv_index * HEAD_DIM:(kv_index + 1) * HEAD_DIM]
        scores = jnp.dot(query_head, key_head.T, precision=highest) * logit_scale
        scores = jnp.where(visible, scores, -1e30)
        largest = jnp.max(scores, axis=1, keepdims=True)
        weights = jnp.where(visible, jnp.exp(scores - largest), 0.0)
        weights = weights / jnp.sum(weights, axis=1, keepdims=True)
        output = jnp.dot(weights, value_head, precision=highest)
        delta_row = jnp.sum(grad_head * output, axis=1, keepdims=True)
        grad_prob = jnp.dot(grad_head, value_head.T, precision=highest)
        grad_score = weights * (grad_prob - delta_row)
        query_grads.append(jnp.dot(grad_score, key_head, precision=highest) * logit_scale)
        key_grads[kv_index] = key_grads[kv_index] + jnp.dot(grad_score.T, query_head, precision=highest) * logit_scale
        value_grads[kv_index] = value_grads[kv_index] + jnp.dot(weights.T, grad_head, precision=highest)
    return jnp.concatenate(query_grads, axis=1), jnp.concatenate(key_grads, axis=1), jnp.concatenate(value_grads, axis=1)


def reference(hidden, queries, out_grad, w_key, w_value, fork_tile, live_len):
    key_rows = jnp.dot(hidden, w_key, precision=highest)
    value_rows = jnp.dot(hidden, w_value, precision=highest)
    kv_width = key_rows.shape[1]
    fork_span = CAP * TILE
    remote_count = N_TOK * fork_span
    path_rows = path_table(fork_tile, N_TOK, TOK_DEV // TILE)
    fork_keys = key_rows.reshape(N_TOK, TOK_DEV, kv_width)[:, :fork_span].reshape(remote_count, kv_width)
    fork_values = value_rows.reshape(N_TOK, TOK_DEV, kv_width)[:, :fork_span].reshape(remote_count, kv_width)

    def per_branch(totals, branch):
        first_row = branch * TOK_DEV
        query_rows = lax.dynamic_slice_in_dim(queries, first_row, TOK_DEV, 0)
        live_rows = (jnp.arange(TOK_DEV) < live_len[branch]).astype(jnp.float32)[:, None]
        grad_rows = lax.dynamic_slice_in_dim(out_grad, first_row, TOK_DEV, 0) * live_rows
        own_keys = lax.dynamic_slice_in_dim(key_rows, first_row, TOK_DEV, 0)
        own_values = lax.dynamic_slice_in_dim(value_rows, first_row, TOK_DEV, 0)
        visible = visible_mask(path_rows[branch], live_len[branch], TOK_DEV, N_TOK)
        grad_q, grad_k, grad_v = attend(query_rows, grad_rows, jnp.concatenate([fork_keys, own_keys], axis=0), jnp.concatenate([fork_values, own_values], axis=0), visible)
        totals = (totals[0] + grad_k[:remote_count], totals[1] + grad_v[:remote_count])
        return totals, (grad_q, grad_k[remote_count:], grad_v[remote_count:])

    initial = (jnp.zeros((remote_count, kv_width), jnp.float32), jnp.zeros((remote_count, kv_width), jnp.float32))
    totals, outputs = lax.scan(per_branch, initial, jnp.arange(N_TOK, dtype=jnp.int32))
    grad_query = outputs[0].reshape(N_TOK * TOK_DEV, -1)
    grad_key = outputs[1].at[:, :fork_span].add(totals[0].reshape(N_TOK, fork_span, kv_width)).reshape(N_TOK * TOK_DEV, kv_width)
    grad_value = outputs[2].at[:, :fork_span].add(totals[1].reshape(N_TOK, fork_span, kv_width)).reshape(N_TOK * TOK_DEV, kv_width)
    grad_w_key = jnp.dot(hidden.T, grad_key, precision=highest)
    grad_w_value = jnp.dot(hidden.T, grad_value, precision=highest)
    return grad_query, grad_key, grad_value, grad_w_key, grad_w_value
```

```python
import functools
import jax, jax.numpy as jnp
from jax import lax
from jax.experimental import pallas as pl
from jax.experimental.pallas import tpu as pltpu
from jax.sharding import Mesh
from jax.sharding import PartitionSpec as P

MESH_ID = pl.DeviceIdType.MESH
RING = 4
OFFSETS = (0, 3, 1, 2)


def turned(axis, by):
    return lax.rem(lax.axis_index(axis) + by, RING)


def greet(axes):
    barrier = pltpu.get_barrier_semaphore()
    for axis in axes:
        for by in (1, 3):
            pl.semaphore_signal(barrier, inc=1, device_id={axis: turned(axis, by)}, device_id_type=MESH_ID)
    pl.semaphore_wait(barrier, 2 * len(axes))


class Wire:
    def __init__(self, send_sem, recv_sem):
        self.send_sem, self.recv_sem, self.sent = send_sem, recv_sem, []

    def copy(self, key, src, dst, axis, by):
        return pltpu.make_async_remote_copy(
            src_ref=src, dst_ref=dst, send_sem=self.send_sem.at[key], recv_sem=self.recv_sem.at[key],
            device_id={axis: turned(axis, by)}, device_id_type=MESH_ID)

    def send(self, key, src, dst, axis, by):
        copy = self.copy(key, src, dst, axis, by)
        copy.start()
        self.sent.append(copy)

    def arrived(self, key, dst, axis, by):
        self.copy(key, dst, dst, axis, by).wait_recv()

    def drain(self):
        for copy in self.sent:
            copy.wait_send()


R0, R1, L0, L1, FR, FL = range(6)


def gather_torus(wire, out, rows):
    quarter = rows // 4
    axes = (("x", "y"), ("y", "x"))

    def slot(half, a, b):
        return a * RING + b if half == 0 else b * RING + a

    def piece(half, a, b, q):
        return out.at[slot(half, a, b), pl.ds((half * 2 + q) * quarter, quarter)]

    def key(half, phase, kind):
        return half * 30 + phase * 6 + kind

    def coords(half, phase, step):
        first, second = axes[half]
        if phase == 0:
            return turned(first, step), lax.axis_index(second)
        return turned(first, OFFSETS[phase - 1]), turned(second, step)

    def ring(half, phase):
        return axes[half][0] if phase == 0 else axes[half][1]

    def send(half, phase, kind, step, q, by):
        part = piece(half, *coords(half, phase, step), q)
        wire.send(key(half, phase, kind), part, part, ring(half, phase), by)

    def arrived(half, phase, kind, step, q):
        part = piece(half, *coords(half, phase, step), q)
        wire.arrived(key(half, phase, kind), part, ring(half, phase), 1)

    def own(phase):
        for kind, q, by in ((R0, 0, 1), (L1, 1, 3), (R1, 1, 1), (L0, 0, 3)):
            for half in (0, 1):
                send(half, phase, kind, 0, q, by)

    def forward(phase):
        for half in (0, 1):
            arrived(half, phase, R0, 3, 0)
            send(half, phase, FR, 3, 0, 1)
            arrived(half, phase, L1, 1, 1)
            send(half, phase, FL, 1, 1, 3)

    def rest(phase):
        for half in (0, 1):
            arrived(half, phase, R1, 3, 1)
            arrived(half, phase, L0, 1, 0)

    def last(phase):
        for half in (0, 1):
            arrived(half, phase, FR, 2, 0)
            arrived(half, phase, FL, 2, 1)

    own(0)
    forward(0)
    own(1)
    rest(0)
    own(2)
    own(3)
    forward(1)
    last(0)
    own(4)
    forward(2)
    forward(3)
    forward(4)
    for phase in (1, 2, 3, 4):
        rest(phase)
        last(phase)


def gather_kernel(rows, own_ref, out_ref, send_sem, recv_sem, local_sem):
    greet(("x", "y"))
    me = lax.axis_index("x") * RING + lax.axis_index("y")
    local = pltpu.make_async_copy(own_ref, out_ref.at[me], local_sem)
    local.start()
    local.wait()
    wire = Wire(send_sem, recv_sem)
    gather_torus(wire, out_ref, rows)
    wire.drain()


def all_gather_plane(own, collective_id):
    rows, cols = own.shape
    return pl.pallas_call(
        functools.partial(gather_kernel, rows),
        out_shape=jax.ShapeDtypeStruct((16, rows, cols), own.dtype),
        in_specs=[pl.BlockSpec(memory_space=pltpu.VMEM)],
        out_specs=pl.BlockSpec(memory_space=pltpu.VMEM),
        scratch_shapes=[pltpu.SemaphoreType.DMA((60,)), pltpu.SemaphoreType.DMA((60,)), pltpu.SemaphoreType.DMA],
        compiler_params=pltpu.CompilerParams(collective_id=collective_id, has_side_effects=True),
    )(own)


S1, S2, S3, T1, T2, T3 = range(6)


def scatter_torus(wire, parts, landing, rows):
    quarter = rows // 4
    axes = (("x", "y"), ("y", "x"))

    def piece(half, a, b, q):
        slot = a * RING + b if half == 0 else b * RING + a
        return parts.at[slot, pl.ds((half * 2 + q) * quarter, quarter)]

    def key(half, phase, kind):
        return half * 30 + phase * 6 + kind

    def ring(half, phase):
        return axes[half][0] if phase == 0 else axes[half][1]

    def part(half, phase, step, q):
        first, second = axes[half]
        if phase == 0:
            return piece(half, turned(first, step), lax.axis_index(second), q)
        return piece(half, turned(first, OFFSETS[phase - 1]), turned(second, step), q)

    def send(half, phase, kind, step, q, by):
        k = key(half, phase, kind)
        wire.send(k, part(half, phase, step, q), landing.at[k], ring(half, phase), by)

    def add(half, phase, kind, step, q):
        k = key(half, phase, kind)
        wire.arrived(k, landing.at[k], ring(half, phase), 1)
        into = part(half, phase, step, q)
        into[...] = into[...] + landing[k]

    def begin(phase):
        for kind, step, q, by in ((S1, 2, 0, 1), (T1, 2, 1, 3), (S2, 1, 1, 1), (T2, 3, 0, 3)):
            for half in (0, 1):
                send(half, phase, kind, step, q, by)

    def relay(phase):
        for half in (0, 1):
            add(half, phase, S1, 1, 0)
            send(half, phase, S3, 1, 0, 1)
            add(half, phase, T1, 3, 1)
            send(half, phase, T3, 3, 1, 3)

    def finish(phase):
        for half in (0, 1):
            add(half, phase, S2, 0, 1)
            add(half, phase, T2, 0, 0)
            add(half, phase, S3, 0, 0)
            add(half, phase, T3, 0, 1)

    begin(4)
    begin(2)
    relay(4)
    begin(3)
    relay(2)
    finish(4)
    begin(1)
    relay(3)
    finish(2)
    relay(1)
    finish(3)
    begin(0)
    relay(0)
    finish(1)
    finish(0)


def scatter_kernel(rows, in_ref, out_ref, parts, landing, send_sem, recv_sem, local_sem):
    greet(("x", "y"))
    me = lax.axis_index("x") * RING + lax.axis_index("y")
    load = pltpu.make_async_copy(in_ref, parts, local_sem)
    load.start()
    load.wait()
    wire = Wire(send_sem, recv_sem)
    scatter_torus(wire, parts, landing, rows)
    wire.drain()
    out_ref[...] = parts[me]


def reduce_scatter_plane(blocks, collective_id):
    _, rows, cols = blocks.shape
    return pl.pallas_call(
        functools.partial(scatter_kernel, rows),
        out_shape=jax.ShapeDtypeStruct((rows, cols), blocks.dtype),
        in_specs=[pl.BlockSpec(memory_space=pl.ANY)],
        out_specs=pl.BlockSpec(memory_space=pltpu.VMEM),
        scratch_shapes=[pltpu.VMEM(blocks.shape, blocks.dtype), pltpu.VMEM((60, rows // 4, cols), blocks.dtype),
                        pltpu.SemaphoreType.DMA((60,)), pltpu.SemaphoreType.DMA((60,)), pltpu.SemaphoreType.DMA],
        compiler_params=pltpu.CompilerParams(collective_id=collective_id, has_side_effects=True),
    )(blocks)


def partner_id():
    return {"core": 1 - lax.axis_index("core")}


def greet_column():
    barrier = pltpu.get_barrier_semaphore()
    for by in (1, 3):
        pl.semaphore_signal(barrier, inc=1, device_id={"z": turned("z", by)}, device_id_type=MESH_ID)
    pl.semaphore_signal(barrier, inc=1, device_id=partner_id(), device_id_type=MESH_ID)
    pl.semaphore_wait(barrier, 3)


def column_gather_kernel(rows, own_ref, out_ref, send_sem, recv_sem, local_sem):
    greet_column()
    core = lax.axis_index("core")
    half = rows // 2

    def piece(step, q, which):
        return out_ref.at[turned("z", step) * 2 + which, pl.ds(q * half, half)]

    local = pltpu.make_async_copy(own_ref, out_ref.at[lax.axis_index("z") * 2 + core], local_sem)
    local.start()
    local.wait()
    wire = Wire(send_sem, recv_sem)

    def over(key, step, q):
        part = piece(step, q, core)
        copy = pltpu.make_async_remote_copy(
            src_ref=part, dst_ref=part, send_sem=send_sem.at[key], recv_sem=recv_sem.at[key],
            device_id=partner_id(), device_id_type=MESH_ID)
        copy.start()
        wire.sent.append(copy)

    def z_send(kind, step, q, by):
        wire.send(kind, piece(step, q, core), piece(step, q, core), "z", by)

    def z_arrived(kind, step, q):
        wire.arrived(kind, piece(step, q, core), "z", 1)
        over(kind + 8, step, q)

    z_send(R0, 0, 0, 1)
    z_send(L1, 0, 1, 3)
    z_send(R1, 0, 1, 1)
    z_send(L0, 0, 0, 3)
    over(6, 0, 0)
    over(7, 0, 1)
    wire.arrived(R0, piece(3, 0, core), "z", 1)
    z_send(FR, 3, 0, 1)
    over(R0 + 8, 3, 0)
    wire.arrived(L1, piece(1, 1, core), "z", 1)
    z_send(FL, 1, 1, 3)
    over(L1 + 8, 1, 1)
    z_arrived(R1, 3, 1)
    z_arrived(L0, 1, 0)
    z_arrived(FR, 2, 0)
    z_arrived(FL, 2, 1)
    other = 1 - core
    for key, step, q in ((6, 0, 0), (7, 0, 1), (R0 + 8, 3, 0), (L1 + 8, 1, 1), (R1 + 8, 3, 1),
                         (L0 + 8, 1, 0), (FR + 8, 2, 0), (FL + 8, 2, 1)):
        wire.arrived(key, piece(step, q, other), "z", 1)
    wire.drain()


def all_gather_column(own, collective_id):
    rows, cols = own.shape
    return pl.pallas_call(
        functools.partial(column_gather_kernel, rows),
        out_shape=jax.ShapeDtypeStruct((8, rows, cols), own.dtype),
        in_specs=[pl.BlockSpec(memory_space=pltpu.VMEM)],
        out_specs=pl.BlockSpec(memory_space=pltpu.VMEM),
        scratch_shapes=[pltpu.SemaphoreType.DMA((14,)), pltpu.SemaphoreType.DMA((14,)), pltpu.SemaphoreType.DMA],
        compiler_params=pltpu.CompilerParams(collective_id=collective_id, has_side_effects=True),
    )(own)


def column_scatter_kernel(rows, in_ref, out_ref, parts, crossed, landing, send_sem, recv_sem, local_sem):
    greet_column()
    core = lax.axis_index("core")
    half = rows // 2
    load = pltpu.make_async_copy(in_ref, parts, local_sem)
    load.start()
    load.wait()
    wire = Wire(send_sem, recv_sem)

    def block(step, which):
        return parts.at[turned("z", step) * 2 + which]

    for i, step in enumerate((2, 1, 3, 0)):
        copy = pltpu.make_async_remote_copy(
            src_ref=block(step, 1 - core), dst_ref=crossed.at[i], send_sem=send_sem.at[6 + i],
            recv_sem=recv_sem.at[6 + i], device_id=partner_id(), device_id_type=MESH_ID)
        copy.start()
        wire.sent.append(copy)

    def cross(i, step):
        wire.arrived(6 + i, crossed.at[i], "z", 1)
        into = block(step, core)
        into[...] = into[...] + crossed[i]

    def part(step, q):
        return parts.at[turned("z", step) * 2 + core, pl.ds(q * half, half)]

    def send(kind, step, q, by):
        wire.send(kind, part(step, q), landing.at[kind], "z", by)

    def add(kind, step, q):
        wire.arrived(kind, landing.at[kind], "z", 1)
        into = part(step, q)
        into[...] = into[...] + landing[kind]

    cross(0, 2)
    send(S1, 2, 0, 1)
    send(T1, 2, 1, 3)
    cross(1, 1)
    send(S2, 1, 1, 1)
    cross(2, 3)
    send(T2, 3, 0, 3)
    add(S1, 1, 0)
    send(S3, 1, 0, 1)
    add(T1, 3, 1)
    send(T3, 3, 1, 3)
    cross(3, 0)
    add(S2, 0, 1)
    add(T2, 0, 0)
    add(S3, 0, 0)
    add(T3, 0, 1)
    wire.drain()
    out_ref[...] = parts[lax.axis_index("z") * 2 + core]


def reduce_scatter_column(blocks, collective_id):
    _, rows, cols = blocks.shape
    return pl.pallas_call(
        functools.partial(column_scatter_kernel, rows),
        out_shape=jax.ShapeDtypeStruct((rows, cols), blocks.dtype),
        in_specs=[pl.BlockSpec(memory_space=pl.ANY)],
        out_specs=pl.BlockSpec(memory_space=pltpu.VMEM),
        scratch_shapes=[pltpu.VMEM(blocks.shape, blocks.dtype), pltpu.VMEM((4, rows, cols), blocks.dtype),
                        pltpu.VMEM((6, rows // 2, cols), blocks.dtype),
                        pltpu.SemaphoreType.DMA((10,)), pltpu.SemaphoreType.DMA((10,)), pltpu.SemaphoreType.DMA],
        compiler_params=pltpu.CompilerParams(collective_id=collective_id, has_side_effects=True),
    )(blocks)


HEAD_DIM = 128
TILE = 128
SPAN = 256
ROWS = 512
BRANCHES = 16
TILE_COUNT = ROWS // TILE
logit_scale = 168.0 ** (-0.5)
HIDDEN_SCORE = -1e30


def split(x, terms):
    parts = []
    for _ in range(terms):
        part = x.astype(jnp.bfloat16)
        parts.append(part)
        x = x - part.astype(jnp.float32)
    return parts


def dot(a, b, contract=((1,), (0,))):
    return lax.dot_general(a, b, (contract, ((), ())), preferred_element_type=jnp.float32)


NT = ((1,), (1,))


def attend_kernel(branch_ref, fork_ref, live_ref, q_ref, g_ref, remote_ref, own_ref,
                  gq_ref, gremote_ref, gown_ref,
                  entry, qcat, gcat, qt, gt, weights, gprob, high, low, delta, gq_acc):
    branch = branch_ref[0]
    live = live_ref[branch]
    for o in range(BRANCHES):
        entry[o] = -1

    def climb(_, b):
        f = fork_ref[jnp.maximum(b - 1, 0)]
        parent = f // TILE_COUNT

        @pl.when(b > 0)
        def _():
            entry[parent] = f % TILE_COUNT

        return jnp.where(b > 0, parent, 0)

    lax.fori_loop(0, BRANCHES - 1, climb, branch)

    both = lambda x: jnp.concatenate([x[:, :HEAD_DIM], x[:, HEAD_DIM:]], axis=0)
    q = both(q_ref[...]) * logit_scale
    q1, q2, q3 = split(q, 3)
    qcat[...] = jnp.concatenate([q1, q1, q2, q2, q1, q3], axis=1)
    qt1, qt2 = split(q.T, 2)
    qt[...] = jnp.concatenate([qt1, qt2], axis=0)
    position = lax.broadcasted_iota(jnp.int32, (2 * ROWS, 1), 0) % ROWS
    g = both(g_ref[...]) * (position < live).astype(jnp.float32)
    g1, g2, g3 = split(g, 3)
    gcat[...] = jnp.concatenate([g1, g1, g2, g2, g1, g3], axis=1)
    gt1, gt2 = split(g.T, 2)
    gt[...] = jnp.concatenate([gt1, gt2], axis=0)
    gremote_ref[...] = jnp.zeros_like(gremote_ref)
    gq_acc[...] = jnp.zeros_like(gq_acc)
    high[...] = jnp.full_like(high, HIDDEN_SCORE)
    low[...] = jnp.zeros_like(low)
    delta[...] = jnp.zeros_like(delta)
    fold = lambda x, op: op(x[:, :HEAD_DIM], x[:, HEAD_DIM:])
    wide = lambda x: jnp.concatenate([x, x], axis=1)

    def remote_key(o):
        return remote_ref[o, :SPAN, :]

    def remote_value(o):
        return remote_ref[o, SPAN:, :]

    def own_key(t):
        return own_ref[t * SPAN : (t + 1) * SPAN, :HEAD_DIM]

    def own_value(t):
        return own_ref[t * SPAN : (t + 1) * SPAN, HEAD_DIM:]

    def over_tiles(visit):
        for t in range(2):
            visit(BRANCHES + t, own_key(t), own_value(t), t)

        def step(o, carry):
            @pl.when(entry[o] >= 0)
            def _():
                visit(o, remote_key(o), remote_value(o), None)

            return carry

        lax.fori_loop(0, BRANCHES, step, 0)

    def score(slot, key, value, own_tile):
        k1, k2, k3 = split(key, 3)
        kcat = jnp.concatenate([k1, k2, k1, k2, k3, k1], axis=1)
        s = dot(qcat[...], kcat, NT)
        column = lax.broadcasted_iota(jnp.int32, (1, SPAN), 1)
        if own_tile is None:
            seen = column // TILE <= entry[slot]
            s = s + jnp.where(seen, 0.0, HIDDEN_SCORE)
        else:
            column = column + own_tile * SPAN
            seen = (column <= position) & (column < live)
            s = jnp.where(seen, s, HIDDEN_SCORE)
        weights[slot] = s
        high[...] = jnp.maximum(high[...], fold(s, jnp.maximum))

    over_tiles(score)
    largest = jnp.max(high[...], axis=1, keepdims=True)
    high[...] = jnp.broadcast_to(largest, high.shape)

    def weigh(slot, key, value, own_tile):
        v1, v2, v3 = split(value, 3)
        gp = dot(gcat[...], jnp.concatenate([v1, v2, v1, v2, v3, v1], axis=1), NT)
        e = jnp.exp(weights[slot] - wide(high[...]))
        weights[slot] = e
        gprob[slot] = gp
        low[...] += fold(e, jnp.add)
        delta[...] += fold(e * gp, jnp.add)

    over_tiles(weigh)
    total = jnp.sum(low[...], axis=1, keepdims=True)
    inverse = 1.0 / total
    low[...] = jnp.broadcast_to(inverse, low.shape)
    delta[...] = jnp.broadcast_to(jnp.sum(delta[...], axis=1, keepdims=True) * inverse, delta.shape)

    def backward(slot, key, value, own_tile):
        p = weights[slot] * wide(low[...])
        ds = p * (gprob[slot] - wide(delta[...]))
        p1, p2 = split(p, 2)
        s1, s2 = split(ds, 2)
        k1, k2 = split(key, 2)
        kk = jnp.concatenate([k1, k2], axis=1)
        gq_acc[...] += dot(s1, kk) + dot(s2, kk)
        gkt = dot(qt[...], s1) + dot(qt[...], s2)
        gvt = dot(gt[...], p1) + dot(gt[...], p2)
        gk = (gkt[:HEAD_DIM] + gkt[HEAD_DIM:]).T
        gv = (gvt[:HEAD_DIM] + gvt[HEAD_DIM:]).T
        if own_tile is None:
            gremote_ref[slot, :SPAN, :] = gk
            gremote_ref[slot, SPAN:, :] = gv
        else:
            gown_ref[own_tile * SPAN : (own_tile + 1) * SPAN, :HEAD_DIM] = gk
            gown_ref[own_tile * SPAN : (own_tile + 1) * SPAN, HEAD_DIM:] = gv

    over_tiles(backward)
    gq = fold(gq_acc[...], jnp.add) * logit_scale
    gq_ref[...] = jnp.concatenate([gq[:ROWS], gq[ROWS:]], axis=1)


def attend(branch, fork_tile, live_len, queries, out_grad, remote, own):
    smem = pl.BlockSpec(memory_space=pltpu.SMEM)
    vmem = pl.BlockSpec(memory_space=pltpu.VMEM)
    f32, bf16 = jnp.float32, jnp.bfloat16
    both = 2 * ROWS
    return pl.pallas_call(
        attend_kernel,
        out_shape=(jax.ShapeDtypeStruct((ROWS, 2 * HEAD_DIM), f32),
                   jax.ShapeDtypeStruct((BRANCHES, 2 * SPAN, HEAD_DIM), f32),
                   jax.ShapeDtypeStruct((ROWS, 2 * HEAD_DIM), f32)),
        in_specs=[smem] * 3 + [vmem] * 4,
        out_specs=[vmem] * 3,
        scratch_shapes=[pltpu.SMEM((BRANCHES,), jnp.int32),
                        pltpu.VMEM((both, 6 * HEAD_DIM), bf16), pltpu.VMEM((both, 6 * HEAD_DIM), bf16),
                        pltpu.VMEM((2 * HEAD_DIM, both), bf16), pltpu.VMEM((2 * HEAD_DIM, both), bf16),
                        pltpu.VMEM((BRANCHES + 2, both, SPAN), f32), pltpu.VMEM((BRANCHES + 2, both, SPAN), f32),
                        pltpu.VMEM((both, HEAD_DIM), f32), pltpu.VMEM((both, HEAD_DIM), f32),
                        pltpu.VMEM((both, HEAD_DIM), f32), pltpu.VMEM((both, 2 * HEAD_DIM), f32)],
        compiler_params=pltpu.CompilerParams(vmem_limit_bytes=64_000_000),
    )(branch, fork_tile, live_len, queries, out_grad, remote, own)


highest = lax.Precision.HIGHEST
HALF = HEAD_DIM // 2


def in_heads(halves):
    return jnp.concatenate(
        [halves[0, :, :HALF], halves[1, :, :HALF], halves[0, :, HALF:], halves[1, :, HALF:]], axis=1
    )


def shards(hidden, queries, out_grad, w_key, w_value, fork_tile, live_len):
    branch = lax.axis_index(("x", "y"))[None].astype(jnp.int32)
    weights = all_gather_plane(jnp.concatenate([w_key, w_value], axis=1), 1)
    partials = jnp.einsum("td,jdc->jtc", hidden, weights, precision=highest)
    own = reduce_scatter_column(partials.reshape(8, 2 * ROWS, HEAD_DIM), 2)
    own = in_heads(own.reshape(2, ROWS, HEAD_DIM))
    fork_rows = jnp.concatenate([own[:SPAN, :HEAD_DIM], own[:SPAN, HEAD_DIM:]], axis=0)
    remote = all_gather_plane(fork_rows, 3)
    grad_query, grad_remote, grad_own = attend(branch, fork_tile, live_len, queries, out_grad, remote, own)
    returned = reduce_scatter_plane(grad_remote, 4)
    grad_own = grad_own.at[:SPAN].add(jnp.concatenate([returned[:SPAN], returned[SPAN:]], axis=1))
    grads = all_gather_column(grad_own, 5)
    blocks = jnp.einsum("htsuc,td->hudsc", grads.reshape(8, ROWS, 2, 2, HALF), hidden, precision=highest)
    summed = reduce_scatter_plane(blocks.reshape(16, hidden.shape[1], HEAD_DIM), 6)
    return (grad_query, grad_own[:, :HEAD_DIM], grad_own[:, HEAD_DIM:], summed[:, :HALF], summed[:, HALF:])


def solution(mesh):
    torus = Mesh(mesh.devices.reshape(4, 4, 4, 2), ("x", "y", "z", "core"))
    tok, head = ("x", "y"), ("z", "core")
    by_both, by_head = P(tok, head), P(head, tok)
    return jax.shard_map(
        shards,
        mesh=torus,
        in_specs=(by_both, by_both, by_both, by_head, by_head, P(), P()),
        out_specs=(by_both, by_both, by_both, by_head, by_head),
        check_vma=False,
    )
```

```python
import functools
import jax, jax.numpy as jnp
from jax import lax
from jax.experimental import pallas as pl
from jax.experimental.pallas import tpu as pltpu
from jax.sharding import Mesh
from jax.sharding import PartitionSpec as P

HEAD_DIM = 128
TILE = 128
SPAN = 256
ROWS = 512
BRANCHES = 16
TILE_COUNT = ROWS // TILE
logit_scale = 168.0 ** (-0.5)
HIDDEN_SCORE = -1e30


MESH_ID = pl.DeviceIdType.MESH
RING = 4
OFFSETS = (0, 3, 1, 2)
PLANE = RING * RING
HALF = HEAD_DIM // 2
CHIP_HEADS = 2
AXES = (("x", "y"), ("y", "x"))


def turned(axis, by):
    return lax.rem(lax.axis_index(axis) + by, RING)


def partner_id():
    return {"core": 1 - lax.axis_index("core")}


def greet():
    barrier = pltpu.get_barrier_semaphore()
    for axis in ("x", "y", "z"):
        for by in (1, 3):
            pl.semaphore_signal(barrier, inc=1, device_id={axis: turned(axis, by)}, device_id_type=MESH_ID)
    pl.semaphore_signal(barrier, inc=1, device_id=partner_id(), device_id_type=MESH_ID)
    pl.semaphore_wait(barrier, 7)


class Wire:
    def __init__(self, send_sem, recv_sem):
        self.send_sem, self.recv_sem, self.sent = send_sem, recv_sem, []

    def copy(self, key, src, dst, device):
        return pltpu.make_async_remote_copy(
            src_ref=src, dst_ref=dst, send_sem=self.send_sem.at[key], recv_sem=self.recv_sem.at[key],
            device_id=device, device_id_type=MESH_ID)

    def send(self, key, src, dst, device):
        copy = self.copy(key, src, dst, device)
        copy.start()
        self.sent.append(copy)

    def arrived(self, key, dst):
        self.copy(key, dst, dst, partner_id()).wait_recv()

    def drain(self):
        for copy in self.sent:
            copy.wait_send()


R0, R1, L0, L1, FR, FL = range(6)
S1, S2, S3, T1, T2, T3 = range(6)


class PlanePieces:
    def __init__(self, wire, blocks, rows):
        self.wire, self.blocks, self.quarter = wire, blocks, rows // 4

    def ring(self, half, phase):
        return AXES[half][0] if phase == 0 else AXES[half][1]

    def piece(self, half, phase, step, q):
        first, second = AXES[half]
        if phase == 0:
            a, b = turned(first, step), lax.axis_index(second)
        else:
            a, b = turned(first, OFFSETS[phase - 1]), turned(second, step)
        slot = a * RING + b if half == 0 else b * RING + a
        return self.blocks.at[slot, pl.ds((half * 2 + q) * self.quarter, self.quarter)]

    def key(self, half, phase, kind):
        return half * 30 + phase * 6 + kind


class PlaneGather(PlanePieces):
    def send(self, half, phase, kind, step, q, by):
        part = self.piece(half, phase, step, q)
        axis = self.ring(half, phase)
        self.wire.send(self.key(half, phase, kind), part, part, {axis: turned(axis, by)})

    def arrived(self, half, phase, kind, step, q):
        self.wire.arrived(self.key(half, phase, kind), self.piece(half, phase, step, q))

    def own(self, phase):
        for kind, q, by in ((R0, 0, 1), (L1, 1, 3), (R1, 1, 1), (L0, 0, 3)):
            for half in (0, 1):
                self.send(half, phase, kind, 0, q, by)

    def forward(self, phase):
        for half in (0, 1):
            self.arrived(half, phase, R0, 3, 0)
            self.send(half, phase, FR, 3, 0, 1)
            self.arrived(half, phase, L1, 1, 1)
            self.send(half, phase, FL, 1, 1, 3)

    def rest(self, phase):
        for half in (0, 1):
            self.arrived(half, phase, R1, 3, 1)
            self.arrived(half, phase, L0, 1, 0)

    def last(self, phase):
        for half in (0, 1):
            self.arrived(half, phase, FR, 2, 0)
            self.arrived(half, phase, FL, 2, 1)

    def run(self, between):
        steps = [
            lambda: self.own(0), lambda: self.forward(0), lambda: self.own(1), lambda: self.rest(0),
            lambda: self.own(2), lambda: self.own(3), lambda: self.forward(1), lambda: self.last(0),
            lambda: self.own(4), lambda: self.forward(2),
            lambda: (self.rest(1), self.last(1)), lambda: self.forward(3),
            lambda: (self.rest(2), self.last(2)), lambda: self.forward(4),
            lambda: (self.rest(3), self.last(3)), lambda: (self.rest(4), self.last(4))]
        for number, step in enumerate(steps):
            step()
            for work in between.get(number, ()):
                work()


class PlaneScatter(PlanePieces):
    def __init__(self, wire, blocks, landing, rows):
        super().__init__(wire, blocks, rows)
        self.landing = landing

    def send(self, half, phase, kind, step, q, by):
        k = self.key(half, phase, kind)
        axis = self.ring(half, phase)
        self.wire.send(k, self.piece(half, phase, step, q), self.landing.at[k], {axis: turned(axis, by)})

    def add(self, half, phase, kind, step, q):
        k = self.key(half, phase, kind)
        self.wire.arrived(k, self.landing.at[k])
        into = self.piece(half, phase, step, q)
        into[...] = into[...] + self.landing[k]

    def begin(self, phase):
        for kind, step, q, by in ((S1, 2, 0, 1), (T1, 2, 1, 3), (S2, 1, 1, 1), (T2, 3, 0, 3)):
            for half in (0, 1):
                self.send(half, phase, kind, step, q, by)

    def relay(self, phase):
        for half in (0, 1):
            self.add(half, phase, S1, 1, 0)
            self.send(half, phase, S3, 1, 0, 1)
            self.add(half, phase, T1, 3, 1)
            self.send(half, phase, T3, 3, 1, 3)

    def finish(self, phase):
        for half in (0, 1):
            self.add(half, phase, S2, 0, 1)
            self.add(half, phase, T2, 0, 0)
            self.add(half, phase, S3, 0, 0)
            self.add(half, phase, T3, 0, 1)

    def run(self, between):
        steps = [
            lambda: self.begin(4), lambda: self.begin(2), lambda: self.relay(4), lambda: self.begin(3),
            lambda: self.relay(2), lambda: self.finish(4), lambda: self.begin(1), lambda: self.relay(3),
            lambda: self.finish(2), lambda: self.relay(1), lambda: self.finish(3), lambda: self.begin(0),
            lambda: self.relay(0), lambda: self.finish(1), lambda: self.finish(0)]
        for number, step in enumerate(steps):
            step()
            for work in between.get(number, ()):
                work()


def head_slot(step, which, q):
    return (turned("z", step) * CHIP_HEADS + which) * 2 + q


class ColumnScatter:
    def __init__(self, wire, base, parts, crossed, landing, start, count):
        self.wire, self.base, self.parts = wire, base, parts
        self.crossed, self.landing, self.rows = crossed, landing, pl.ds(start, count)

    def cross_begin(self):
        other = 1 - lax.axis_index("core")
        for i, step in enumerate((2, 1, 3, 0)):
            src = self.parts.at[pl.ds(head_slot(step, other, 0), 2), self.rows]
            self.wire.send(self.base + 6 + i, src, self.crossed.at[i], partner_id())

    def crossed_in(self, i, step):
        self.wire.arrived(self.base + 6 + i, self.crossed.at[i])
        into = self.parts.at[pl.ds(head_slot(step, lax.axis_index("core"), 0), 2), self.rows]
        into[...] = into[...] + self.crossed[i]

    def part(self, step, q):
        return self.parts.at[head_slot(step, lax.axis_index("core"), q), self.rows]

    def send(self, kind, step, q, by):
        self.wire.send(self.base + kind, self.part(step, q), self.landing.at[kind], {"z": turned("z", by)})

    def add(self, kind, step, q):
        self.wire.arrived(self.base + kind, self.landing.at[kind])
        into = self.part(step, q)
        into[...] = into[...] + self.landing[kind]

    def begin(self):
        self.crossed_in(0, 2)
        self.send(S1, 2, 0, 1)
        self.send(T1, 2, 1, 3)
        self.crossed_in(1, 1)
        self.send(S2, 1, 1, 1)
        self.crossed_in(2, 3)
        self.send(T2, 3, 0, 3)

    def relay(self):
        self.add(S1, 1, 0)
        self.send(S3, 1, 0, 1)
        self.add(T1, 3, 1)
        self.send(T3, 3, 1, 3)
        self.crossed_in(3, 0)

    def finish(self):
        self.add(S2, 0, 1)
        self.add(T2, 0, 0)
        self.add(S3, 0, 0)
        self.add(T3, 0, 1)


class ColumnGather:
    def __init__(self, wire, base, grads, start, count):
        self.wire, self.base, self.grads, self.rows = wire, base, grads, pl.ds(start, count)
        self.core = lax.axis_index("core")

    def part(self, step, q, which):
        return self.grads.at[head_slot(step, which, q), self.rows]

    def along(self, kind, step, q, by):
        part = self.part(step, q, self.core)
        self.wire.send(self.base + kind, part, part, {"z": turned("z", by)})

    def across(self, key, step, q):
        part = self.part(step, q, self.core)
        self.wire.send(self.base + key, part, part, partner_id())

    def begin(self):
        self.along(R0, 0, 0, 1)
        self.along(L1, 0, 1, 3)
        self.along(R1, 0, 1, 1)
        self.along(L0, 0, 0, 3)
        self.across(12, 0, 0)
        self.across(13, 0, 1)

    def forward(self):
        self.wire.arrived(self.base + R0, self.part(3, 0, self.core))
        self.along(FR, 3, 0, 1)
        self.across(6 + R0, 3, 0)
        self.wire.arrived(self.base + L1, self.part(1, 1, self.core))
        self.along(FL, 1, 1, 3)
        self.across(6 + L1, 1, 1)

    def near(self):
        for kind, step, q in ((R1, 3, 1), (L0, 1, 0)):
            self.wire.arrived(self.base + kind, self.part(step, q, self.core))
            self.across(6 + kind, step, q)

    def far(self):
        for kind, step, q in ((FR, 2, 0), (FL, 2, 1)):
            self.wire.arrived(self.base + kind, self.part(step, q, self.core))
            self.across(6 + kind, step, q)

    def partner(self, keys):
        for key, step, q in keys:
            self.wire.arrived(self.base + key, self.part(step, q, 1 - self.core))


def split(x, terms):
    parts = []
    for _ in range(terms):
        part = x.astype(jnp.bfloat16)
        parts.append(part)
        x = x - part.astype(jnp.float32)
    return parts


def dot(a, b, contract=((1,), (0,))):
    return lax.dot_general(a, b, (contract, ((), ())), preferred_element_type=jnp.float32)


NT = ((1,), (1,))


def attend_kernel(branch_ref, fork_ref, live_ref, q_ref, g_ref, remote_ref, own_ref,
                  gq_ref, gremote_ref, gown_ref,
                  entry, qcat, gcat, qt, gt, weights, gprob, high, low, delta, gq_acc):
    branch = branch_ref[0]
    live = live_ref[branch]
    for o in range(BRANCHES):
        entry[o] = -1

    def climb(_, b):
        f = fork_ref[jnp.maximum(b - 1, 0)]
        parent = f // TILE_COUNT

        @pl.when(b > 0)
        def _():
            entry[parent] = f % TILE_COUNT

        return jnp.where(b > 0, parent, 0)

    lax.fori_loop(0, BRANCHES - 1, climb, branch)

    both = lambda x: jnp.concatenate([x[:, :HEAD_DIM], x[:, HEAD_DIM:]], axis=0)
    q = both(q_ref[...]) * logit_scale
    q1, q2, q3 = split(q, 3)
    qcat[...] = jnp.concatenate([q1, q1, q2, q2, q1, q3], axis=1)
    qt1, qt2 = split(q.T, 2)
    qt[...] = jnp.concatenate([qt1, qt2], axis=0)
    position = lax.broadcasted_iota(jnp.int32, (2 * ROWS, 1), 0) % ROWS
    g = both(g_ref[...]) * (position < live).astype(jnp.float32)
    g1, g2, g3 = split(g, 3)
    gcat[...] = jnp.concatenate([g1, g1, g2, g2, g1, g3], axis=1)
    gt1, gt2 = split(g.T, 2)
    gt[...] = jnp.concatenate([gt1, gt2], axis=0)
    gremote_ref[...] = jnp.zeros_like(gremote_ref)
    gq_acc[...] = jnp.zeros_like(gq_acc)
    high[...] = jnp.full_like(high, HIDDEN_SCORE)
    low[...] = jnp.zeros_like(low)
    delta[...] = jnp.zeros_like(delta)
    fold = lambda x, op: op(x[:, :HEAD_DIM], x[:, HEAD_DIM:])
    wide = lambda x: jnp.concatenate([x, x], axis=1)

    def remote_key(o):
        return remote_ref[o, :SPAN, :]

    def remote_value(o):
        return remote_ref[o, SPAN:, :]

    def own_key(t):
        return own_ref[t * SPAN : (t + 1) * SPAN, :HEAD_DIM]

    def own_value(t):
        return own_ref[t * SPAN : (t + 1) * SPAN, HEAD_DIM:]

    def over_tiles(visit):
        for t in range(2):
            visit(BRANCHES + t, own_key(t), own_value(t), t)

        def step(o, carry):
            @pl.when(entry[o] >= 0)
            def _():
                visit(o, remote_key(o), remote_value(o), None)

            return carry

        lax.fori_loop(0, BRANCHES, step, 0)

    def score(slot, key, value, own_tile):
        k1, k2, k3 = split(key, 3)
        kcat = jnp.concatenate([k1, k2, k1, k2, k3, k1], axis=1)
        s = dot(qcat[...], kcat, NT)
        column = lax.broadcasted_iota(jnp.int32, (1, SPAN), 1)
        if own_tile is None:
            seen = column // TILE <= entry[slot]
            s = s + jnp.where(seen, 0.0, HIDDEN_SCORE)
        else:
            column = column + own_tile * SPAN
            seen = (column <= position) & (column < live)
            s = jnp.where(seen, s, HIDDEN_SCORE)
        weights[slot] = s
        high[...] = jnp.maximum(high[...], fold(s, jnp.maximum))

    over_tiles(score)
    largest = jnp.max(high[...], axis=1, keepdims=True)
    high[...] = jnp.broadcast_to(largest, high.shape)

    def weigh(slot, key, value, own_tile):
        v1, v2, v3 = split(value, 3)
        gp = dot(gcat[...], jnp.concatenate([v1, v2, v1, v2, v3, v1], axis=1), NT)
        e = jnp.exp(weights[slot] - wide(high[...]))
        weights[slot] = e
        gprob[slot] = gp
        low[...] += fold(e, jnp.add)
        delta[...] += fold(e * gp, jnp.add)

    over_tiles(weigh)
    total = jnp.sum(low[...], axis=1, keepdims=True)
    inverse = 1.0 / total
    low[...] = jnp.broadcast_to(inverse, low.shape)
    delta[...] = jnp.broadcast_to(jnp.sum(delta[...], axis=1, keepdims=True) * inverse, delta.shape)

    def backward(slot, key, value, own_tile):
        p = weights[slot] * wide(low[...])
        ds = p * (gprob[slot] - wide(delta[...]))
        p1, p2 = split(p, 2)
        s1, s2 = split(ds, 2)
        k1, k2 = split(key, 2)
        kk = jnp.concatenate([k1, k2], axis=1)
        gq_acc[...] += dot(s1, kk) + dot(s2, kk)
        gkt = dot(qt[...], s1) + dot(qt[...], s2)
        gvt = dot(gt[...], p1) + dot(gt[...], p2)
        gk = (gkt[:HEAD_DIM] + gkt[HEAD_DIM:]).T
        gv = (gvt[:HEAD_DIM] + gvt[HEAD_DIM:]).T
        if own_tile is None:
            gremote_ref[slot, :SPAN, :] = gk
            gremote_ref[slot, SPAN:, :] = gv
        else:
            gown_ref[own_tile * SPAN : (own_tile + 1) * SPAN, :HEAD_DIM] = gk
            gown_ref[own_tile * SPAN : (own_tile + 1) * SPAN, HEAD_DIM:] = gv

    over_tiles(backward)
    gq = fold(gq_acc[...], jnp.add) * logit_scale
    gq_ref[...] = jnp.concatenate([gq[:ROWS], gq[ROWS:]], axis=1)


def attend(branch, fork_tile, live_len, queries, out_grad, remote, own):
    smem = pl.BlockSpec(memory_space=pltpu.SMEM)
    vmem = pl.BlockSpec(memory_space=pltpu.VMEM)
    f32, bf16 = jnp.float32, jnp.bfloat16
    both = 2 * ROWS
    return pl.pallas_call(
        attend_kernel,
        out_shape=(jax.ShapeDtypeStruct((ROWS, 2 * HEAD_DIM), f32),
                   jax.ShapeDtypeStruct((BRANCHES, 2 * SPAN, HEAD_DIM), f32),
                   jax.ShapeDtypeStruct((ROWS, 2 * HEAD_DIM), f32)),
        in_specs=[smem] * 3 + [vmem] * 4,
        out_specs=[vmem] * 3,
        scratch_shapes=[pltpu.SMEM((BRANCHES,), jnp.int32),
                        pltpu.VMEM((both, 6 * HEAD_DIM), bf16), pltpu.VMEM((both, 6 * HEAD_DIM), bf16),
                        pltpu.VMEM((2 * HEAD_DIM, both), bf16), pltpu.VMEM((2 * HEAD_DIM, both), bf16),
                        pltpu.VMEM((BRANCHES + 2, both, SPAN), f32), pltpu.VMEM((BRANCHES + 2, both, SPAN), f32),
                        pltpu.VMEM((both, HEAD_DIM), f32), pltpu.VMEM((both, HEAD_DIM), f32),
                        pltpu.VMEM((both, HEAD_DIM), f32), pltpu.VMEM((both, 2 * HEAD_DIM), f32)],
        compiler_params=pltpu.CompilerParams(vmem_limit_bytes=64_000_000),
    )(branch, fork_tile, live_len, queries, out_grad, remote, own)


def project_kernel(own_ref, hidden_ref, kv_ref, remote_ref,
                   weights, hidden, left, parts, crossed, landing,
                   plane_send, plane_recv, fork_send, fork_recv, column_send, column_recv, local_sem):
    depth = hidden_ref.shape[1]
    half_depth = depth // 2
    me = lax.axis_index("x") * RING + lax.axis_index("y")
    local = pltpu.make_async_copy(own_ref, weights.at[me], local_sem.at[0])
    local.start()
    rows_in = pltpu.make_async_copy(hidden_ref, hidden, local_sem.at[1])
    rows_in.start()
    greet()
    local.wait()

    def prepare():
        rows_in.wait()
        for half in (0, 1):
            h1, h2, h3 = split(hidden[:, half * half_depth : (half + 1) * half_depth], 3)
            left[half] = jnp.concatenate([h1, h1, h2, h2, h1, h3], axis=1)
        parts[...] = jnp.zeros_like(parts)

    def project(phase, half):
        other = turned(AXES[half][0], OFFSETS[phase - 1])
        slots = [other * RING + i if half == 0 else i * RING + other for i in range(RING)]
        rows = slice(half * half_depth, (half + 1) * half_depth)
        w1, w2, w3 = split(jnp.concatenate([weights[slot, rows, :] for slot in slots], axis=1), 3)
        product = dot(left[half], jnp.concatenate([w1, w2, w1, w2, w3, w1], axis=0))
        for i, slot in enumerate(slots):
            parts[slot] += product[:, i * HEAD_DIM : (i + 1) * HEAD_DIM]

    def both_halves(phase):
        return [functools.partial(project, phase, half) for half in (0, 1)]

    wire = Wire(plane_send, plane_recv)
    PlaneGather(wire, weights, depth).run(
        {0: [prepare], 10: both_halves(1), 12: both_halves(2), 14: both_halves(3), 15: both_halves(4)})

    column = Wire(column_send, column_recv)
    fork, tail = [
        ColumnScatter(column, 10 * i, parts, crossed.at[i], landing.at[i], i * SPAN, SPAN) for i in range(2)]
    fork.cross_begin()
    tail.cross_begin()
    fork.begin()
    fork.relay()
    fork.finish()

    def in_heads(start):
        first, second = [parts[head_slot(0, lax.axis_index("core"), q), start : start + SPAN] for q in range(2)]
        return (jnp.concatenate([first[:, :HALF], second[:, :HALF]], axis=1),
                jnp.concatenate([first[:, HALF:], second[:, HALF:]], axis=1))

    keys, values = in_heads(0)
    remote_ref[me, :SPAN] = keys
    remote_ref[me, SPAN:] = values
    kv_ref[:SPAN] = jnp.concatenate([keys, values], axis=1)
    fork_wire = Wire(fork_send, fork_recv)
    PlaneGather(fork_wire, remote_ref, 2 * SPAN).run(
        {0: [tail.begin], 5: [tail.relay], 9: [tail.finish]})
    keys, values = in_heads(SPAN)
    kv_ref[SPAN:] = jnp.concatenate([keys, values], axis=1)
    for used in (wire, column, fork_wire):
        used.drain()


def project_and_share(own_weights, hidden):
    depth = hidden.shape[1]
    f32, bf16 = jnp.float32, jnp.bfloat16
    dma = pltpu.SemaphoreType.DMA
    return pl.pallas_call(
        project_kernel,
        out_shape=(jax.ShapeDtypeStruct((ROWS, 2 * HEAD_DIM), f32),
                   jax.ShapeDtypeStruct((PLANE, 2 * SPAN, HEAD_DIM), f32)),
        in_specs=[pl.BlockSpec(memory_space=pl.ANY)] * 2,
        out_specs=[pl.BlockSpec(memory_space=pltpu.VMEM)] * 2,
        scratch_shapes=[pltpu.VMEM((PLANE, depth, HEAD_DIM), f32), pltpu.VMEM((ROWS, depth), f32),
                        pltpu.VMEM((2, ROWS, 3 * depth), bf16), pltpu.VMEM((PLANE, ROWS, HEAD_DIM), f32),
                        pltpu.VMEM((2, 4, 2, SPAN, HEAD_DIM), f32), pltpu.VMEM((2, 6, SPAN, HEAD_DIM), f32),
                        dma((60,)), dma((60,)), dma((60,)), dma((60,)), dma((20,)), dma((20,)), dma((2,))],
        compiler_params=pltpu.CompilerParams(
            collective_id=1, has_side_effects=True, vmem_limit_bytes=60_000_000),
    )(own_weights, hidden)


def weight_grad_kernel(remote_ref, own_ref, hidden_ref, key_ref, value_ref, grad_ref,
                       returned, landing, grads, hidden, left, blocks, block_landing,
                       plane_send, plane_recv, block_send, block_recv, column_send, column_recv, local_sem):
    depth = hidden_ref.shape[1]
    me = lax.axis_index("x") * RING + lax.axis_index("y")
    core = lax.axis_index("core")
    load = pltpu.make_async_copy(remote_ref, returned, local_sem.at[0])
    load.start()
    rows_in = pltpu.make_async_copy(hidden_ref, hidden, local_sem.at[1])
    rows_in.start()

    def place(start, keys, values):
        rows = slice(start, start + SPAN)
        for q in range(2):
            part = slice(q * HALF, (q + 1) * HALF)
            grads[head_slot(0, core, q), rows] = jnp.concatenate([keys[:, part], values[:, part]], axis=1)
        key_ref[rows] = keys
        value_ref[rows] = values

    place(SPAN, own_ref[SPAN:, :HEAD_DIM], own_ref[SPAN:, HEAD_DIM:])
    greet()
    load.wait()
    column = Wire(column_send, column_recv)
    fork, tail = [ColumnGather(column, 14 * i, grads, i * SPAN, SPAN) for i in range(2)]

    def prepare():
        rows_in.wait()
        for i in range(2):
            h1, h2, h3 = split(hidden[i * SPAN : (i + 1) * SPAN, :].T, 3)
            left[i] = jnp.concatenate([h1, h1, h2, h2, h1, h3], axis=1)

    def multiply(i, step, which):
        rows = pl.ds(i * SPAN, SPAN)
        slot = head_slot(step, which, 0)
        g1, g2, g3 = split(jnp.concatenate([grads[slot, rows, :], grads[slot + 1, rows, :]], axis=1), 3)
        product = dot(left[i], jnp.concatenate([g1, g2, g1, g2, g3, g1], axis=0))
        for q in range(2):
            new = product[:, q * HEAD_DIM : (q + 1) * HEAD_DIM]
            if i == 0:
                blocks[slot + q] += new
            else:
                blocks[slot + q] = new

    own_keys = ((12, 0, 0), (13, 0, 1))
    near_keys = ((6 + R0, 3, 0), (6 + R1, 3, 1), (6 + L0, 1, 0), (6 + L1, 1, 1))
    far_keys = ((6 + FR, 2, 0), (6 + FL, 2, 1))

    def tail_near():
        tail.near()
        multiply(1, 0, core)
        tail.partner(own_keys)
        multiply(1, 0, 1 - core)
        multiply(1, 3, core)

    def tail_far():
        tail.far()
        multiply(1, 1, core)
        tail.partner(near_keys)
        multiply(1, 3, 1 - core)

    def tail_done():
        multiply(1, 1, 1 - core)
        multiply(1, 2, core)
        tail.partner(far_keys)
        multiply(1, 2, 1 - core)

    plane = Wire(plane_send, plane_recv)
    PlaneScatter(plane, returned, landing, 2 * SPAN).run(
        {0: [tail.begin], 1: [prepare], 2: [tail.forward], 4: [tail_near], 6: [tail_far], 8: [tail_done]})
    place(0, own_ref[:SPAN, :HEAD_DIM] + returned[me, :SPAN], own_ref[:SPAN, HEAD_DIM:] + returned[me, SPAN:])
    fork.begin()
    multiply(0, 0, core)
    fork.forward()
    fork.partner(own_keys)
    multiply(0, 0, 1 - core)
    fork.near()
    multiply(0, 3, core)
    fork.far()
    multiply(0, 1, core)
    fork.partner(near_keys)
    multiply(0, 3, 1 - core)
    multiply(0, 1, 1 - core)
    multiply(0, 2, core)
    fork.partner(far_keys)
    multiply(0, 2, 1 - core)
    block_wire = Wire(block_send, block_recv)
    PlaneScatter(block_wire, blocks, block_landing, depth).run({})
    grad_ref[...] = blocks[me]
    for used in (plane, column, block_wire):
        used.drain()


def weight_grads(grad_remote, grad_own, hidden):
    depth = hidden.shape[1]
    f32, bf16 = jnp.float32, jnp.bfloat16
    dma = pltpu.SemaphoreType.DMA
    anywhere, vmem = pl.BlockSpec(memory_space=pl.ANY), pl.BlockSpec(memory_space=pltpu.VMEM)
    return pl.pallas_call(
        weight_grad_kernel,
        out_shape=(jax.ShapeDtypeStruct((ROWS, HEAD_DIM), f32), jax.ShapeDtypeStruct((ROWS, HEAD_DIM), f32),
                   jax.ShapeDtypeStruct((depth, HEAD_DIM), f32)),
        in_specs=[anywhere, vmem, anywhere],
        out_specs=[vmem] * 3,
        scratch_shapes=[pltpu.VMEM((PLANE, 2 * SPAN, HEAD_DIM), f32), pltpu.VMEM((60, SPAN // 2, HEAD_DIM), f32),
                        pltpu.VMEM((PLANE, ROWS, HEAD_DIM), f32), pltpu.VMEM((ROWS, depth), f32),
                        pltpu.VMEM((2, depth, 6 * SPAN), bf16), pltpu.VMEM((PLANE, depth, HEAD_DIM), f32),
                        pltpu.VMEM((60, depth // 4, HEAD_DIM), f32),
                        dma((60,)), dma((60,)), dma((60,)), dma((60,)), dma((28,)), dma((28,)), dma((2,))],
        compiler_params=pltpu.CompilerParams(
            collective_id=2, has_side_effects=True, vmem_limit_bytes=60_000_000),
    )(grad_remote, grad_own, hidden)


def shards(hidden, queries, out_grad, w_key, w_value, fork_tile, live_len):
    branch = lax.axis_index(("x", "y"))[None].astype(jnp.int32)
    own, remote = project_and_share(jnp.concatenate([w_key, w_value], axis=1), hidden)
    grad_query, grad_remote, grad_own = attend(branch, fork_tile, live_len, queries, out_grad, remote, own)
    grad_key, grad_value, grad_weights = weight_grads(grad_remote, grad_own, hidden)
    return (grad_query, grad_key, grad_value, grad_weights[:, :HALF], grad_weights[:, HALF:])


def solution(mesh):
    torus = Mesh(mesh.devices.reshape(4, 4, 4, 2), ("x", "y", "z", "core"))
    tok, head = ("x", "y"), ("z", "core")
    by_both, by_head = P(tok, head), P(head, tok)
    return jax.shard_map(
        shards,
        mesh=torus,
        in_specs=(by_both, by_both, by_both, by_head, by_head, P(), P()),
        out_specs=(by_both, by_both, by_both, by_head, by_head),
        check_vma=False,
    )
```

```python
import functools
import jax, jax.numpy as jnp
from jax import lax
from jax.experimental import pallas as pl
from jax.experimental.pallas import tpu as pltpu
from jax.sharding import Mesh
from jax.sharding import PartitionSpec as P

HEAD_DIM = 128
TILE = 128
SPAN = 256
ROWS = 512
BRANCHES = 16
TILE_COUNT = ROWS // TILE
logit_scale = 168.0 ** (-0.5)
HIDDEN_SCORE = -1e30


MESH_ID = pl.DeviceIdType.MESH
RING = 4
OFFSETS = (0, 3, 1, 2)
PLANE = RING * RING
HALF = HEAD_DIM // 2
CHIP_HEADS = 2
AXES = (("x", "y"), ("y", "x"))


def turned(axis, by):
    return lax.rem(lax.axis_index(axis) + by, RING)


def partner_id():
    return {"core": 1 - lax.axis_index("core")}


def greet():
    barrier = pltpu.get_barrier_semaphore()
    for axis in ("x", "y", "z"):
        for by in (1, 3):
            pl.semaphore_signal(barrier, inc=1, device_id={axis: turned(axis, by)}, device_id_type=MESH_ID)
    pl.semaphore_signal(barrier, inc=1, device_id=partner_id(), device_id_type=MESH_ID)
    pl.semaphore_wait(barrier, 7)


class Wire:
    def __init__(self, send_sem, recv_sem):
        self.send_sem, self.recv_sem, self.sent = send_sem, recv_sem, []

    def copy(self, key, src, dst, device):
        return pltpu.make_async_remote_copy(
            src_ref=src, dst_ref=dst, send_sem=self.send_sem.at[key], recv_sem=self.recv_sem.at[key],
            device_id=device, device_id_type=MESH_ID)

    def send(self, key, src, dst, device):
        copy = self.copy(key, src, dst, device)
        copy.start()
        self.sent.append(copy)

    def arrived(self, key, dst):
        self.copy(key, dst, dst, partner_id()).wait_recv()

    def drain(self):
        for copy in self.sent:
            copy.wait_send()


R0, R1, L0, L1, FR, FL = range(6)
S1, S2, S3, T1, T2, T3 = range(6)


class PlanePieces:
    def __init__(self, wire, blocks, rows):
        self.wire, self.blocks, self.quarter = wire, blocks, rows // 4

    def ring(self, half, phase):
        return AXES[half][0] if phase == 0 else AXES[half][1]

    def piece(self, half, phase, step, q):
        first, second = AXES[half]
        if phase == 0:
            a, b = turned(first, step), lax.axis_index(second)
        else:
            a, b = turned(first, OFFSETS[phase - 1]), turned(second, step)
        slot = a * RING + b if half == 0 else b * RING + a
        return self.blocks.at[slot, pl.ds((half * 2 + q) * self.quarter, self.quarter)]

    def key(self, half, phase, kind):
        return half * 30 + phase * 6 + kind


class PlaneGather(PlanePieces):
    def send(self, half, phase, kind, step, q, by):
        part = self.piece(half, phase, step, q)
        axis = self.ring(half, phase)
        self.wire.send(self.key(half, phase, kind), part, part, {axis: turned(axis, by)})

    def arrived(self, half, phase, kind, step, q):
        self.wire.arrived(self.key(half, phase, kind), self.piece(half, phase, step, q))

    def own(self, phase):
        for kind, q, by in ((R0, 0, 1), (L1, 1, 3), (R1, 1, 1), (L0, 0, 3)):
            for half in (0, 1):
                self.send(half, phase, kind, 0, q, by)

    def forward(self, phase):
        for half in (0, 1):
            self.arrived(half, phase, R0, 3, 0)
            self.send(half, phase, FR, 3, 0, 1)
            self.arrived(half, phase, L1, 1, 1)
            self.send(half, phase, FL, 1, 1, 3)

    def rest(self, phase):
        for half in (0, 1):
            self.arrived(half, phase, R1, 3, 1)
            self.arrived(half, phase, L0, 1, 0)

    def last(self, phase):
        for half in (0, 1):
            self.arrived(half, phase, FR, 2, 0)
            self.arrived(half, phase, FL, 2, 1)

    def run(self, between):
        steps = [
            lambda: self.own(0), lambda: self.forward(0), lambda: self.own(1), lambda: self.rest(0),
            lambda: self.own(2), lambda: self.own(3), lambda: self.forward(1), lambda: self.last(0),
            lambda: self.own(4), lambda: self.forward(2),
            lambda: (self.rest(1), self.last(1)), lambda: self.forward(3),
            lambda: (self.rest(2), self.last(2)), lambda: self.forward(4),
            lambda: (self.rest(3), self.last(3)), lambda: (self.rest(4), self.last(4))]
        for number, step in enumerate(steps):
            step()
            for work in between.get(number, ()):
                work()


class PlaneScatter(PlanePieces):
    def __init__(self, wire, blocks, landing, rows):
        super().__init__(wire, blocks, rows)
        self.landing = landing

    def send(self, half, phase, kind, step, q, by):
        k = self.key(half, phase, kind)
        axis = self.ring(half, phase)
        self.wire.send(k, self.piece(half, phase, step, q), self.landing.at[k], {axis: turned(axis, by)})

    def add(self, half, phase, kind, step, q):
        k = self.key(half, phase, kind)
        self.wire.arrived(k, self.landing.at[k])
        into = self.piece(half, phase, step, q)
        into[...] = into[...] + self.landing[k]

    def begin(self, phase):
        for kind, step, q, by in ((S1, 2, 0, 1), (T1, 2, 1, 3), (S2, 1, 1, 1), (T2, 3, 0, 3)):
            for half in (0, 1):
                self.send(half, phase, kind, step, q, by)

    def relay(self, phase):
        for half in (0, 1):
            self.add(half, phase, S1, 1, 0)
            self.send(half, phase, S3, 1, 0, 1)
            self.add(half, phase, T1, 3, 1)
            self.send(half, phase, T3, 3, 1, 3)

    def finish(self, phase):
        for half in (0, 1):
            self.add(half, phase, S2, 0, 1)
            self.add(half, phase, T2, 0, 0)
            self.add(half, phase, S3, 0, 0)
            self.add(half, phase, T3, 0, 1)

    def run(self, between):
        steps = [
            lambda: self.begin(4), lambda: self.begin(2), lambda: self.relay(4), lambda: self.begin(3),
            lambda: self.relay(2), lambda: self.finish(4), lambda: self.begin(1), lambda: self.relay(3),
            lambda: self.finish(2), lambda: self.relay(1), lambda: self.finish(3), lambda: self.begin(0),
            lambda: self.relay(0), lambda: self.finish(1), lambda: self.finish(0)]
        for number, step in enumerate(steps):
            step()
            for work in between.get(number, ()):
                work()


def head_slot(step, which, q):
    return (turned("z", step) * CHIP_HEADS + which) * 2 + q


class ColumnScatter:
    def __init__(self, wire, base, parts, crossed, landing, start, count):
        self.wire, self.base, self.parts = wire, base, parts
        self.crossed, self.landing, self.rows = crossed, landing, pl.ds(start, count)

    def cross_begin(self):
        other = 1 - lax.axis_index("core")
        for i, step in enumerate((2, 1, 3, 0)):
            src = self.parts.at[pl.ds(head_slot(step, other, 0), 2), self.rows]
            self.wire.send(self.base + 6 + i, src, self.crossed.at[i], partner_id())

    def crossed_in(self, i, step):
        self.wire.arrived(self.base + 6 + i, self.crossed.at[i])
        into = self.parts.at[pl.ds(head_slot(step, lax.axis_index("core"), 0), 2), self.rows]
        into[...] = into[...] + self.crossed[i]

    def part(self, step, q):
        return self.parts.at[head_slot(step, lax.axis_index("core"), q), self.rows]

    def send(self, kind, step, q, by):
        self.wire.send(self.base + kind, self.part(step, q), self.landing.at[kind], {"z": turned("z", by)})

    def add(self, kind, step, q):
        self.wire.arrived(self.base + kind, self.landing.at[kind])
        into = self.part(step, q)
        into[...] = into[...] + self.landing[kind]

    def begin(self):
        self.crossed_in(0, 2)
        self.send(S1, 2, 0, 1)
        self.send(T1, 2, 1, 3)
        self.crossed_in(1, 1)
        self.send(S2, 1, 1, 1)
        self.crossed_in(2, 3)
        self.send(T2, 3, 0, 3)

    def relay(self):
        self.add(S1, 1, 0)
        self.send(S3, 1, 0, 1)
        self.add(T1, 3, 1)
        self.send(T3, 3, 1, 3)
        self.crossed_in(3, 0)

    def finish(self):
        self.add(S2, 0, 1)
        self.add(T2, 0, 0)
        self.add(S3, 0, 0)
        self.add(T3, 0, 1)


class ColumnGather:
    def __init__(self, wire, base, grads, start, count):
        self.wire, self.base, self.grads, self.rows = wire, base, grads, pl.ds(start, count)
        self.core = lax.axis_index("core")

    def part(self, step, q, which):
        return self.grads.at[head_slot(step, which, q), self.rows]

    def along(self, kind, step, q, by):
        part = self.part(step, q, self.core)
        self.wire.send(self.base + kind, part, part, {"z": turned("z", by)})

    def across(self, key, step, q):
        part = self.part(step, q, self.core)
        self.wire.send(self.base + key, part, part, partner_id())

    def begin(self):
        self.along(R0, 0, 0, 1)
        self.along(L1, 0, 1, 3)
        self.along(R1, 0, 1, 1)
        self.along(L0, 0, 0, 3)
        self.across(12, 0, 0)
        self.across(13, 0, 1)

    def forward(self):
        self.wire.arrived(self.base + R0, self.part(3, 0, self.core))
        self.along(FR, 3, 0, 1)
        self.across(6 + R0, 3, 0)
        self.wire.arrived(self.base + L1, self.part(1, 1, self.core))
        self.along(FL, 1, 1, 3)
        self.across(6 + L1, 1, 1)

    def near(self):
        for kind, step, q in ((R1, 3, 1), (L0, 1, 0)):
            self.wire.arrived(self.base + kind, self.part(step, q, self.core))
            self.across(6 + kind, step, q)

    def far(self):
        for kind, step, q in ((FR, 2, 0), (FL, 2, 1)):
            self.wire.arrived(self.base + kind, self.part(step, q, self.core))
            self.across(6 + kind, step, q)

    def partner(self, keys):
        for key, step, q in keys:
            self.wire.arrived(self.base + key, self.part(step, q, 1 - self.core))


def split(x, terms):
    parts = []
    for _ in range(terms):
        part = x.astype(jnp.bfloat16)
        parts.append(part)
        x = x - part.astype(jnp.float32)
    return parts


def dot(a, b, contract=((1,), (0,))):
    return lax.dot_general(a, b, (contract, ((), ())), preferred_element_type=jnp.float32)


NT = ((1,), (1,))


def attend_kernel(branch_ref, fork_ref, live_ref, q_ref, g_ref, remote_hbm, own_ref,
                  gq_ref, gremote_hbm, gtail_ref,
                  entry, remote, gremote, qcat, gcat, qt, gt, weights, gprob, high, low, delta, gq_acc,
                  in_sem, out_sem):
    branch = branch_ref[0]
    live = live_ref[branch]

    def load(o):
        return pltpu.make_async_copy(remote_hbm.at[o], remote.at[o], in_sem.at[o])

    def store(o):
        return pltpu.make_async_copy(gremote.at[o], gremote_hbm.at[o], out_sem.at[o])

    for o in range(BRANCHES):
        load(o).start()
        entry[o] = -1

    def climb(_, b):
        f = fork_ref[jnp.maximum(b - 1, 0)]
        parent = f // TILE_COUNT

        @pl.when(b > 0)
        def _():
            entry[parent] = f % TILE_COUNT

        return jnp.where(b > 0, parent, 0)

    lax.fori_loop(0, BRANCHES - 1, climb, branch)

    both = lambda x: jnp.concatenate([x[:, :HEAD_DIM], x[:, HEAD_DIM:]], axis=0)
    q = both(q_ref[...]) * logit_scale
    q1, q2, q3 = split(q, 3)
    qcat[...] = jnp.concatenate([q1, q1, q2, q2, q1, q3], axis=1)
    qt1, qt2 = split(q.T, 2)
    qt[...] = jnp.concatenate([qt1, qt2], axis=0)
    position = lax.broadcasted_iota(jnp.int32, (2 * ROWS, 1), 0) % ROWS
    g = both(g_ref[...]) * (position < live).astype(jnp.float32)
    g1, g2, g3 = split(g, 3)
    gcat[...] = jnp.concatenate([g1, g1, g2, g2, g1, g3], axis=1)
    gt1, gt2 = split(g.T, 2)
    gt[...] = jnp.concatenate([gt1, gt2], axis=0)
    gq_acc[...] = jnp.zeros_like(gq_acc)
    high[...] = jnp.full_like(high, HIDDEN_SCORE)
    low[...] = jnp.zeros_like(low)
    delta[...] = jnp.zeros_like(delta)
    fold = lambda x, op: op(x[:, :HEAD_DIM], x[:, HEAD_DIM:])
    wide = lambda x: jnp.concatenate([x, x], axis=1)

    def over_tiles(visit, before=None, after=None):
        for t in range(2):
            rows = slice(t * SPAN, (t + 1) * SPAN)
            visit(BRANCHES + t, lambda: own_ref[rows, :HEAD_DIM], lambda: own_ref[rows, HEAD_DIM:], t)

        def step(o, carry):
            if before is not None:
                before(o)

            @pl.when(entry[o] >= 0)
            def _():
                visit(o, lambda: remote[o, :SPAN, :], lambda: remote[o, SPAN:, :], None)

            if after is not None:
                after(o)
            return carry

        lax.fori_loop(0, BRANCHES, step, 0)

    def score(slot, key, value, own_tile):
        k1, k2, k3 = split(key(), 3)
        s = dot(qcat[...], jnp.concatenate([k1, k2, k1, k2, k3, k1], axis=1), NT)
        column = lax.broadcasted_iota(jnp.int32, (1, SPAN), 1)
        if own_tile is None:
            s = s + jnp.where(column // TILE <= entry[slot], 0.0, HIDDEN_SCORE)
        else:
            column = column + own_tile * SPAN
            s = jnp.where((column <= position) & (column < live), s, HIDDEN_SCORE)
        weights[slot] = s
        high[...] = jnp.maximum(high[...], fold(s, jnp.maximum))

    over_tiles(score, before=lambda o: load(o).wait())
    high[...] = jnp.broadcast_to(jnp.max(high[...], axis=1, keepdims=True), high.shape)

    def weigh(slot, key, value, own_tile):
        v1, v2, v3 = split(value(), 3)
        gp = dot(gcat[...], jnp.concatenate([v1, v2, v1, v2, v3, v1], axis=1), NT)
        e = jnp.exp(weights[slot] - wide(high[...]))
        weights[slot] = e
        gprob[slot] = gp
        low[...] += fold(e, jnp.add)
        delta[...] += fold(e * gp, jnp.add)

    over_tiles(weigh)
    inverse = 1.0 / jnp.sum(low[...], axis=1, keepdims=True)
    low[...] = jnp.broadcast_to(inverse, low.shape)
    delta[...] = jnp.broadcast_to(jnp.sum(delta[...], axis=1, keepdims=True) * inverse, delta.shape)

    def backward(slot, key, value, own_tile):
        p = weights[slot] * wide(low[...])
        ds = p * (gprob[slot] - wide(delta[...]))
        p1, p2 = split(p, 2)
        s1, s2 = split(ds, 2)
        k1, k2 = split(key(), 2)
        kk = jnp.concatenate([k1, k2], axis=1)
        gq_acc[...] += dot(s1, kk) + dot(s2, kk)
        gkt = dot(qt[...], s1) + dot(qt[...], s2)
        gvt = dot(gt[...], p1) + dot(gt[...], p2)
        gk = (gkt[:HEAD_DIM] + gkt[HEAD_DIM:]).T
        gv = (gvt[:HEAD_DIM] + gvt[HEAD_DIM:]).T
        if own_tile == 1:
            gtail_ref[:SPAN, :] = gk
            gtail_ref[SPAN:, :] = gv
        else:
            row = branch if own_tile == 0 else slot
            gremote[row, :SPAN, :] = gk
            gremote[row, SPAN:, :] = gv

    def unseen(o):
        @pl.when((entry[o] < 0) & (o != branch))
        def _():
            gremote[o] = jnp.zeros((2 * SPAN, HEAD_DIM), jnp.float32)

    over_tiles(backward, before=unseen, after=lambda o: store(o).start())
    gq = fold(gq_acc[...], jnp.add) * logit_scale
    gq_ref[...] = jnp.concatenate([gq[:ROWS], gq[ROWS:]], axis=1)
    for o in range(BRANCHES):
        store(o).wait()


def attend(branch, fork_tile, live_len, queries, out_grad, remote, own):
    smem = pl.BlockSpec(memory_space=pltpu.SMEM)
    vmem = pl.BlockSpec(memory_space=pltpu.VMEM)
    anywhere = pl.BlockSpec(memory_space=pl.ANY)
    f32, bf16 = jnp.float32, jnp.bfloat16
    both = 2 * ROWS
    block = (2 * SPAN, HEAD_DIM)
    return pl.pallas_call(
        attend_kernel,
        out_shape=(jax.ShapeDtypeStruct((ROWS, 2 * HEAD_DIM), f32),
                   jax.ShapeDtypeStruct((BRANCHES,) + block, f32),
                   jax.ShapeDtypeStruct(block, f32)),
        in_specs=[smem] * 3 + [vmem] * 2 + [anywhere, vmem],
        out_specs=[vmem, anywhere, vmem],
        scratch_shapes=[pltpu.SMEM((BRANCHES,), jnp.int32),
                        pltpu.VMEM((BRANCHES,) + block, f32), pltpu.VMEM((BRANCHES,) + block, f32),
                        pltpu.VMEM((both, 6 * HEAD_DIM), bf16), pltpu.VMEM((both, 6 * HEAD_DIM), bf16),
                        pltpu.VMEM((2 * HEAD_DIM, both), bf16), pltpu.VMEM((2 * HEAD_DIM, both), bf16),
                        pltpu.VMEM((BRANCHES + 2, both, SPAN), f32), pltpu.VMEM((BRANCHES + 2, both, SPAN), f32),
                        pltpu.VMEM((both, HEAD_DIM), f32), pltpu.VMEM((both, HEAD_DIM), f32),
                        pltpu.VMEM((both, HEAD_DIM), f32), pltpu.VMEM((both, 2 * HEAD_DIM), f32),
                        pltpu.SemaphoreType.DMA((BRANCHES,)), pltpu.SemaphoreType.DMA((BRANCHES,))],
        compiler_params=pltpu.CompilerParams(vmem_limit_bytes=64_000_000),
    )(branch, fork_tile, live_len, queries, out_grad, remote, own)


def project_kernel(w_key_ref, w_value_ref, hidden_ref, kv_ref, remote_ref,
                   weights, hidden, left, parts, crossed, landing,
                   plane_send, plane_recv, fork_send, fork_recv, column_send, column_recv,
                   local_sem):
    depth = hidden_ref.shape[0]
    half_depth = depth // 2
    me = lax.axis_index("x") * RING + lax.axis_index("y")
    rows_in = pltpu.make_async_copy(hidden_ref, hidden, local_sem.at[0])
    rows_in.start()
    weights[me] = jnp.concatenate([w_key_ref[...], w_value_ref[...]], axis=0).T
    greet()

    def prepare():
        rows_in.wait()
        for half in (0, 1):
            h1, h2, h3 = split(hidden[half * half_depth : (half + 1) * half_depth, :].T, 3)
            left[half] = jnp.concatenate([h1, h1, h2, h2, h1, h3], axis=1)
        parts[...] = jnp.zeros_like(parts)

    def project(phase, half):
        other = turned(AXES[half][0], OFFSETS[phase - 1])
        slots = [other * RING + i if half == 0 else i * RING + other for i in range(RING)]
        rows = slice(half * half_depth, (half + 1) * half_depth)
        w1, w2, w3 = split(jnp.concatenate([weights[slot, rows, :] for slot in slots], axis=1), 3)
        product = dot(left[half], jnp.concatenate([w1, w2, w1, w2, w3, w1], axis=0))
        for i, slot in enumerate(slots):
            parts[slot] += product[:, i * HEAD_DIM : (i + 1) * HEAD_DIM]

    def both_halves(phase):
        return [functools.partial(project, phase, half) for half in (0, 1)]

    wire = Wire(plane_send, plane_recv)
    PlaneGather(wire, weights, depth).run(
        {0: [prepare], 10: both_halves(1), 12: both_halves(2), 14: both_halves(3), 15: both_halves(4)})

    column = Wire(column_send, column_recv)
    fork, tail = [
        ColumnScatter(column, 10 * i, parts, crossed.at[i], landing.at[i], i * SPAN, SPAN) for i in range(2)]
    fork.cross_begin()
    tail.cross_begin()
    fork.begin()
    fork.relay()
    fork.finish()

    def in_heads(start):
        first, second = [parts[head_slot(0, lax.axis_index("core"), q), start : start + SPAN] for q in range(2)]
        return (jnp.concatenate([first[:, :HALF], second[:, :HALF]], axis=1),
                jnp.concatenate([first[:, HALF:], second[:, HALF:]], axis=1))

    keys, values = in_heads(0)
    remote_ref[me, :SPAN] = keys
    remote_ref[me, SPAN:] = values
    kv_ref[:SPAN] = jnp.concatenate([keys, values], axis=1)
    fork_wire = Wire(fork_send, fork_recv)
    PlaneGather(fork_wire, remote_ref, 2 * SPAN).run(
        {0: [tail.begin], 5: [tail.relay], 9: [tail.finish]})
    keys, values = in_heads(SPAN)
    kv_ref[SPAN:] = jnp.concatenate([keys, values], axis=1)
    for used in (wire, column, fork_wire):
        used.drain()


def project_and_share(w_key, w_value, hidden):
    depth = hidden.shape[0]
    f32, bf16 = jnp.float32, jnp.bfloat16
    dma = pltpu.SemaphoreType.DMA
    return pl.pallas_call(
        project_kernel,
        out_shape=(jax.ShapeDtypeStruct((ROWS, 2 * HEAD_DIM), f32),
                   jax.ShapeDtypeStruct((PLANE, 2 * SPAN, HEAD_DIM), f32)),
        in_specs=[pl.BlockSpec(memory_space=pltpu.VMEM)] * 2 + [pl.BlockSpec(memory_space=pl.ANY)],
        out_specs=[pl.BlockSpec(memory_space=pltpu.VMEM)] * 2,
        scratch_shapes=[pltpu.VMEM((PLANE, depth, HEAD_DIM), f32), pltpu.VMEM((depth, ROWS), f32),
                        pltpu.VMEM((2, ROWS, 3 * depth), bf16), pltpu.VMEM((PLANE, ROWS, HEAD_DIM), f32),
                        pltpu.VMEM((2, 4, 2, SPAN, HEAD_DIM), f32), pltpu.VMEM((2, 6, SPAN, HEAD_DIM), f32),
                        dma((60,)), dma((60,)), dma((60,)), dma((60,)), dma((20,)), dma((20,)), dma((1,))],
        compiler_params=pltpu.CompilerParams(
            collective_id=1, has_side_effects=True, vmem_limit_bytes=60_000_000),
    )(w_key, w_value, hidden)


def weight_grad_kernel(remote_ref, tail_ref, hidden_ref, key_ref, value_ref, grad_ref,
                       returned, landing, grads, hidden, left, blocks, block_landing,
                       plane_send, plane_recv, block_send, block_recv, column_send, column_recv,
                       local_sem):
    depth = hidden_ref.shape[0]
    me = lax.axis_index("x") * RING + lax.axis_index("y")
    core = lax.axis_index("core")
    load = pltpu.make_async_copy(remote_ref, returned, local_sem.at[0])
    load.start()
    rows_in = pltpu.make_async_copy(hidden_ref, hidden, local_sem.at[1])
    rows_in.start()

    def place(start, keys, values):
        rows = slice(start, start + SPAN)
        for q in range(2):
            part = slice(q * HALF, (q + 1) * HALF)
            grads[head_slot(0, core, q), rows] = jnp.concatenate([keys[:, part], values[:, part]], axis=1)
        key_ref[rows] = keys
        value_ref[rows] = values

    place(SPAN, tail_ref[:SPAN], tail_ref[SPAN:])
    greet()
    load.wait()
    column = Wire(column_send, column_recv)
    fork, tail = [ColumnGather(column, 14 * i, grads, i * SPAN, SPAN) for i in range(2)]

    def prepare():
        rows_in.wait()
        for i in range(2):
            h1, h2, h3 = split(hidden[:, i * SPAN : (i + 1) * SPAN], 3)
            left[i] = jnp.concatenate([h1, h1, h2, h2, h1, h3], axis=1)

    def multiply(i, step, which):
        rows = pl.ds(i * SPAN, SPAN)
        slot = head_slot(step, which, 0)
        g1, g2, g3 = split(jnp.concatenate([grads[slot, rows, :], grads[slot + 1, rows, :]], axis=1), 3)
        product = dot(left[i], jnp.concatenate([g1, g2, g1, g2, g3, g1], axis=0))
        for q in range(2):
            new = product[:, q * HEAD_DIM : (q + 1) * HEAD_DIM]
            if i == 0:
                blocks[slot + q] += new
            else:
                blocks[slot + q] = new

    own_keys = ((12, 0, 0), (13, 0, 1))
    near_keys = ((6 + R0, 3, 0), (6 + R1, 3, 1), (6 + L0, 1, 0), (6 + L1, 1, 1))
    far_keys = ((6 + FR, 2, 0), (6 + FL, 2, 1))

    def tail_near():
        tail.near()
        multiply(1, 0, core)
        tail.partner(own_keys)
        multiply(1, 0, 1 - core)
        multiply(1, 3, core)

    def tail_far():
        tail.far()
        multiply(1, 1, core)
        tail.partner(near_keys)
        multiply(1, 3, 1 - core)

    def tail_done():
        multiply(1, 1, 1 - core)
        multiply(1, 2, core)
        tail.partner(far_keys)
        multiply(1, 2, 1 - core)

    plane = Wire(plane_send, plane_recv)
    PlaneScatter(plane, returned, landing, 2 * SPAN).run(
        {0: [tail.begin], 1: [prepare], 2: [tail.forward], 4: [tail_near], 6: [tail_far], 8: [tail_done]})
    place(0, returned[me, :SPAN], returned[me, SPAN:])
    fork.begin()

    multiply(0, 0, core)
    fork.forward()
    fork.partner(own_keys)
    multiply(0, 0, 1 - core)
    fork.near()
    multiply(0, 3, core)
    fork.far()
    multiply(0, 1, core)
    fork.partner(near_keys)
    multiply(0, 3, 1 - core)
    multiply(0, 1, 1 - core)
    multiply(0, 2, core)
    fork.partner(far_keys)
    multiply(0, 2, 1 - core)
    block_wire = Wire(block_send, block_recv)
    PlaneScatter(block_wire, blocks, block_landing, depth).run({})
    grad_ref[...] = blocks[me].T
    for used in (plane, column, block_wire):
        used.drain()


def weight_grads(grad_remote, grad_tail, hidden):
    depth = hidden.shape[0]
    f32, bf16 = jnp.float32, jnp.bfloat16
    dma = pltpu.SemaphoreType.DMA
    anywhere, vmem = pl.BlockSpec(memory_space=pl.ANY), pl.BlockSpec(memory_space=pltpu.VMEM)
    return pl.pallas_call(
        weight_grad_kernel,
        out_shape=(jax.ShapeDtypeStruct((ROWS, HEAD_DIM), f32), jax.ShapeDtypeStruct((ROWS, HEAD_DIM), f32),
                   jax.ShapeDtypeStruct((HEAD_DIM, depth), f32)),
        in_specs=[anywhere, vmem, anywhere],
        out_specs=[vmem] * 3,
        scratch_shapes=[pltpu.VMEM((PLANE, 2 * SPAN, HEAD_DIM), f32), pltpu.VMEM((60, SPAN // 2, HEAD_DIM), f32),
                        pltpu.VMEM((PLANE, ROWS, HEAD_DIM), f32), pltpu.VMEM((depth, ROWS), f32),
                        pltpu.VMEM((2, depth, 6 * SPAN), bf16), pltpu.VMEM((PLANE, depth, HEAD_DIM), f32),
                        pltpu.VMEM((60, depth // 4, HEAD_DIM), f32),
                        dma((60,)), dma((60,)), dma((60,)), dma((60,)), dma((28,)), dma((28,)),
                        dma((2,))],
        compiler_params=pltpu.CompilerParams(
            collective_id=2, has_side_effects=True, vmem_limit_bytes=60_000_000),
    )(grad_remote, grad_tail, hidden)


def results_kernel(key_in, value_in, weights_in, key_ref, value_ref, w_key_ref, w_value_ref):
    key_ref[...] = key_in[...]
    value_ref[...] = value_in[...]
    w_key_ref[...] = weights_in[:HALF]
    w_value_ref[...] = weights_in[HALF:]


def results(key, value, weights):
    f32 = jnp.float32
    vmem = pl.BlockSpec(memory_space=pltpu.VMEM)
    half = jax.ShapeDtypeStruct((HALF, weights.shape[1]), f32)
    return pl.pallas_call(
        results_kernel,
        out_shape=(jax.ShapeDtypeStruct(key.shape, f32), jax.ShapeDtypeStruct(value.shape, f32), half, half),
        in_specs=[vmem] * 3,
        out_specs=[vmem] * 4,
    )(key, value, weights)


def shards(hidden, queries, out_grad, w_key, w_value, fork_tile, live_len):
    branch = lax.axis_index(("x", "y"))[None].astype(jnp.int32)
    own, remote = project_and_share(w_key.T, w_value.T, hidden.T)
    gq, gremote, gtail = attend(branch, fork_tile, live_len, queries, out_grad, remote, own)
    key, value, gw_key, gw_value = results(*weight_grads(gremote, gtail, hidden.T))
    return gq, key, value, gw_key.T, gw_value.T


def solution(mesh):
    torus = Mesh(mesh.devices.reshape(4, 4, 4, 2), ("x", "y", "z", "core"))
    tok, head = ("x", "y"), ("z", "core")
    by_both, by_head = P(tok, head), P(head, tok)
    return jax.shard_map(
        shards,
        mesh=torus,
        in_specs=(by_both, by_both, by_both, by_head, by_head, P(), P()),
        out_specs=(by_both, by_both, by_both, by_head, by_head),
        check_vma=False,
    )
```

```python
import functools
import jax, jax.numpy as jnp
from jax import lax
from jax.experimental import pallas as pl
from jax.experimental.pallas import tpu as pltpu
from jax.sharding import Mesh
from jax.sharding import PartitionSpec as P

HEAD_DIM = 128
TILE = 128
SPAN = 256
ROWS = 512
BRANCHES = 16
TILE_COUNT = ROWS // TILE
logit_scale = 168.0 ** (-0.5)
HIDDEN_SCORE = -1e30


MESH_ID = pl.DeviceIdType.MESH
RING = 4
OFFSETS = (0, 3, 1, 2)
PLANE = RING * RING
HALF = HEAD_DIM // 2
CHIP_HEADS = 2
AXES = (("x", "y"), ("y", "x"))


def turned(axis, by):
    return lax.rem(lax.axis_index(axis) + by, RING)


def partner_id():
    return {"core": 1 - lax.axis_index("core")}


def greet():
    barrier = pltpu.get_barrier_semaphore()
    for axis in ("x", "y", "z"):
        for by in (1, 3):
            pl.semaphore_signal(barrier, inc=1, device_id={axis: turned(axis, by)}, device_id_type=MESH_ID)
    pl.semaphore_signal(barrier, inc=1, device_id=partner_id(), device_id_type=MESH_ID)
    pl.semaphore_wait(barrier, 7)


class Wire:
    def __init__(self, send_sem, recv_sem):
        self.send_sem, self.recv_sem, self.sent = send_sem, recv_sem, []

    def copy(self, key, src, dst, device):
        return pltpu.make_async_remote_copy(
            src_ref=src, dst_ref=dst, send_sem=self.send_sem.at[key], recv_sem=self.recv_sem.at[key],
            device_id=device, device_id_type=MESH_ID)

    def send(self, key, src, dst, device):
        copy = self.copy(key, src, dst, device)
        copy.start()
        self.sent.append(copy)

    def arrived(self, key, dst):
        self.copy(key, dst, dst, partner_id()).wait_recv()

    def drain(self):
        for copy in self.sent:
            copy.wait_send()


R0, R1, L0, L1, FR, FL = range(6)
S1, S2, S3, T1, T2, T3 = range(6)


class PlanePieces:
    def __init__(self, wire, blocks, rows):
        self.wire, self.blocks, self.quarter = wire, blocks, rows // 4

    def ring(self, half, phase):
        return AXES[half][0] if phase == 0 else AXES[half][1]

    def piece(self, half, phase, step, q):
        first, second = AXES[half]
        if phase == 0:
            a, b = turned(first, step), lax.axis_index(second)
        else:
            a, b = turned(first, OFFSETS[phase - 1]), turned(second, step)
        slot = a * RING + b if half == 0 else b * RING + a
        return self.blocks.at[slot, pl.ds((half * 2 + q) * self.quarter, self.quarter)]

    def key(self, half, phase, kind):
        return half * 30 + phase * 6 + kind


class PlaneGather(PlanePieces):
    def send(self, half, phase, kind, step, q, by):
        part = self.piece(half, phase, step, q)
        axis = self.ring(half, phase)
        self.wire.send(self.key(half, phase, kind), part, part, {axis: turned(axis, by)})

    def arrived(self, half, phase, kind, step, q):
        self.wire.arrived(self.key(half, phase, kind), self.piece(half, phase, step, q))

    def own(self, phase):
        for kind, q, by in ((R0, 0, 1), (L1, 1, 3), (R1, 1, 1), (L0, 0, 3)):
            for half in (0, 1):
                self.send(half, phase, kind, 0, q, by)

    def forward(self, phase):
        for half in (0, 1):
            self.arrived(half, phase, R0, 3, 0)
            self.send(half, phase, FR, 3, 0, 1)
            self.arrived(half, phase, L1, 1, 1)
            self.send(half, phase, FL, 1, 1, 3)

    def rest(self, phase):
        for half in (0, 1):
            self.arrived(half, phase, R1, 3, 1)
            self.arrived(half, phase, L0, 1, 0)

    def last(self, phase):
        for half in (0, 1):
            self.arrived(half, phase, FR, 2, 0)
            self.arrived(half, phase, FL, 2, 1)

    def run(self, between):
        steps = [
            lambda: self.own(0), lambda: self.forward(0), lambda: self.own(1), lambda: self.rest(0),
            lambda: self.own(2), lambda: self.own(3), lambda: self.forward(1), lambda: self.last(0),
            lambda: self.own(4), lambda: self.forward(2),
            lambda: (self.rest(1), self.last(1)), lambda: self.forward(3),
            lambda: (self.rest(2), self.last(2)), lambda: self.forward(4),
            lambda: (self.rest(3), self.last(3)), lambda: (self.rest(4), self.last(4))]
        for number, step in enumerate(steps):
            step()
            for work in between.get(number, ()):
                work()


class PlaneScatter(PlanePieces):
    def __init__(self, wire, blocks, landing, rows):
        super().__init__(wire, blocks, rows)
        self.landing = landing

    def send(self, half, phase, kind, step, q, by):
        k = self.key(half, phase, kind)
        axis = self.ring(half, phase)
        self.wire.send(k, self.piece(half, phase, step, q), self.landing.at[k], {axis: turned(axis, by)})

    def add(self, half, phase, kind, step, q):
        k = self.key(half, phase, kind)
        self.wire.arrived(k, self.landing.at[k])
        into = self.piece(half, phase, step, q)
        into[...] = into[...] + self.landing[k]

    def begin_far(self, phase):
        for kind, step, q, by in ((S1, 2, 0, 1), (T1, 2, 1, 3)):
            for half in (0, 1):
                self.send(half, phase, kind, step, q, by)

    def begin_near(self, phase):
        for kind, step, q, by in ((S2, 1, 1, 1), (T2, 3, 0, 3)):
            for half in (0, 1):
                self.send(half, phase, kind, step, q, by)

    def begin(self, phase):
        self.begin_far(phase)
        self.begin_near(phase)

    def relay(self, phase):
        for half in (0, 1):
            self.add(half, phase, S1, 1, 0)
            self.send(half, phase, S3, 1, 0, 1)
            self.add(half, phase, T1, 3, 1)
            self.send(half, phase, T3, 3, 1, 3)

    def finish(self, phase):
        for half in (0, 1):
            self.add(half, phase, S2, 0, 1)
            self.add(half, phase, T2, 0, 0)
            self.add(half, phase, S3, 0, 0)
            self.add(half, phase, T3, 0, 1)

    def run(self, between):
        steps = [
            lambda: self.begin(4), lambda: self.begin(2), lambda: self.relay(4), lambda: self.begin(3),
            lambda: self.relay(2), lambda: (self.finish(4), self.begin_far(0)), lambda: self.relay(3),
            lambda: self.begin(1), lambda: self.finish(2), lambda: (self.finish(3), self.begin_near(0)),
            lambda: self.relay(0), lambda: self.relay(1), lambda: self.finish(1), lambda: self.finish(0)]
        for number, step in enumerate(steps):
            step()
            for work in between.get(number, ()):
                work()


def head_slot(step, which, q):
    return (turned("z", step) * CHIP_HEADS + which) * 2 + q


class ColumnScatter:
    def __init__(self, wire, base, parts, crossed, landing, start, count):
        self.wire, self.base, self.parts = wire, base, parts
        self.crossed, self.landing, self.rows = crossed, landing, pl.ds(start, count)

    def cross_begin(self):
        other = 1 - lax.axis_index("core")
        for i, step in enumerate((2, 1, 3, 0)):
            src = self.parts.at[pl.ds(head_slot(step, other, 0), 2), self.rows]
            self.wire.send(self.base + 6 + i, src, self.crossed.at[i], partner_id())

    def crossed_in(self, i, step):
        self.wire.arrived(self.base + 6 + i, self.crossed.at[i])
        into = self.parts.at[pl.ds(head_slot(step, lax.axis_index("core"), 0), 2), self.rows]
        into[...] = into[...] + self.crossed[i]

    def part(self, step, q):
        return self.parts.at[head_slot(step, lax.axis_index("core"), q), self.rows]

    def send(self, kind, step, q, by):
        self.wire.send(self.base + kind, self.part(step, q), self.landing.at[kind], {"z": turned("z", by)})

    def add(self, kind, step, q):
        self.wire.arrived(self.base + kind, self.landing.at[kind])
        into = self.part(step, q)
        into[...] = into[...] + self.landing[kind]

    def begin(self):
        self.crossed_in(0, 2)
        self.send(S1, 2, 0, 1)
        self.send(T1, 2, 1, 3)
        self.crossed_in(1, 1)
        self.send(S2, 1, 1, 1)
        self.crossed_in(2, 3)
        self.send(T2, 3, 0, 3)

    def relay(self):
        self.add(S1, 1, 0)
        self.send(S3, 1, 0, 1)
        self.add(T1, 3, 1)
        self.send(T3, 3, 1, 3)
        self.crossed_in(3, 0)

    def finish(self):
        self.add(S2, 0, 1)
        self.add(T2, 0, 0)
        self.add(S3, 0, 0)
        self.add(T3, 0, 1)


class ColumnGather:
    def __init__(self, wire, base, grads, start, count):
        self.wire, self.base, self.grads, self.rows = wire, base, grads, pl.ds(start, count)
        self.core = lax.axis_index("core")

    def part(self, step, q, which):
        return self.grads.at[head_slot(step, which, q), self.rows]

    def along(self, kind, step, q, by):
        part = self.part(step, q, self.core)
        self.wire.send(self.base + kind, part, part, {"z": turned("z", by)})

    def across(self, key, step, q):
        part = self.part(step, q, self.core)
        self.wire.send(self.base + key, part, part, partner_id())

    def begin(self):
        self.along(R0, 0, 0, 1)
        self.along(L1, 0, 1, 3)
        self.along(R1, 0, 1, 1)
        self.along(L0, 0, 0, 3)
        self.across(12, 0, 0)
        self.across(13, 0, 1)

    def forward(self):
        self.wire.arrived(self.base + R0, self.part(3, 0, self.core))
        self.along(FR, 3, 0, 1)
        self.across(6 + R0, 3, 0)
        self.wire.arrived(self.base + L1, self.part(1, 1, self.core))
        self.along(FL, 1, 1, 3)
        self.across(6 + L1, 1, 1)

    def near(self):
        for kind, step, q in ((R1, 3, 1), (L0, 1, 0)):
            self.wire.arrived(self.base + kind, self.part(step, q, self.core))
            self.across(6 + kind, step, q)

    def far(self):
        for kind, step, q in ((FR, 2, 0), (FL, 2, 1)):
            self.wire.arrived(self.base + kind, self.part(step, q, self.core))
            self.across(6 + kind, step, q)

    def partner(self, keys):
        for key, step, q in keys:
            self.wire.arrived(self.base + key, self.part(step, q, 1 - self.core))


def split(x, terms):
    parts = []
    for _ in range(terms):
        part = x.astype(jnp.bfloat16)
        parts.append(part)
        x = x - part.astype(jnp.float32)
    return parts


def dot(a, b, contract=((1,), (0,))):
    return lax.dot_general(a, b, (contract, ((), ())), preferred_element_type=jnp.float32)


NT = ((1,), (1,))


def attend_kernel(branch_ref, fork_ref, live_ref, q_ref, g_ref, remote_hbm, own_ref,
                  gq_ref, gremote_hbm, gtail_ref,
                  entry, remote, gremote, qcat, gcat, qt, gt, weights, gprob, high, low, delta, gq_acc,
                  in_sem, out_sem):
    branch = branch_ref[0]
    live = live_ref[branch]

    def load(o):
        return pltpu.make_async_copy(remote_hbm.at[o], remote.at[o], in_sem.at[o])

    def store(o):
        return pltpu.make_async_copy(gremote.at[o], gremote_hbm.at[o], out_sem.at[o])

    for o in range(BRANCHES):
        load(o).start()
        entry[o] = -1

    def climb(_, b):
        f = fork_ref[jnp.maximum(b - 1, 0)]
        parent = f // TILE_COUNT

        @pl.when(b > 0)
        def _():
            entry[parent] = f % TILE_COUNT

        return jnp.where(b > 0, parent, 0)

    lax.fori_loop(0, BRANCHES - 1, climb, branch)

    both = lambda x: jnp.concatenate([x[:, :HEAD_DIM], x[:, HEAD_DIM:]], axis=0)
    q = both(q_ref[...]) * logit_scale
    q1, q2, q3 = split(q, 3)
    qcat[...] = jnp.concatenate([q1, q1, q2, q2, q1, q3], axis=1)
    qt1, qt2 = split(q.T, 2)
    qt[...] = jnp.concatenate([qt1, qt2], axis=0)
    position = lax.broadcasted_iota(jnp.int32, (2 * ROWS, 1), 0) % ROWS
    g = both(g_ref[...]) * (position < live).astype(jnp.float32)
    g1, g2, g3 = split(g, 3)
    gcat[...] = jnp.concatenate([g1, g1, g2, g2, g1, g3], axis=1)
    gt1, gt2 = split(g.T, 2)
    gt[...] = jnp.concatenate([gt1, gt2], axis=0)
    gq_acc[...] = jnp.zeros_like(gq_acc)
    high[...] = jnp.full_like(high, HIDDEN_SCORE)
    low[...] = jnp.zeros_like(low)
    delta[...] = jnp.zeros_like(delta)
    fold = lambda x, op: op(x[:, :HEAD_DIM], x[:, HEAD_DIM:])
    wide = lambda x: jnp.concatenate([x, x], axis=1)

    def over_tiles(visit, before=None, after=None):
        for t in range(2):
            rows = slice(t * SPAN, (t + 1) * SPAN)
            visit(BRANCHES + t, lambda: own_ref[rows, :HEAD_DIM], lambda: own_ref[rows, HEAD_DIM:], t)

        def step(o, carry):
            if before is not None:
                before(o)

            @pl.when(entry[o] >= 0)
            def _():
                visit(o, lambda: remote[o, :SPAN, :], lambda: remote[o, SPAN:, :], None)

            if after is not None:
                after(o)
            return carry

        lax.fori_loop(0, BRANCHES, step, 0)

    def score(slot, key, value, own_tile):
        k1, k2, k3 = split(key(), 3)
        s = dot(qcat[...], jnp.concatenate([k1, k2, k1, k2, k3, k1], axis=1), NT)
        column = lax.broadcasted_iota(jnp.int32, (1, SPAN), 1)
        if own_tile is None:
            s = s + jnp.where(column // TILE <= entry[slot], 0.0, HIDDEN_SCORE)
        else:
            column = column + own_tile * SPAN
            s = jnp.where((column <= position) & (column < live), s, HIDDEN_SCORE)
        weights[slot] = s
        high[...] = jnp.maximum(high[...], fold(s, jnp.maximum))

    over_tiles(score, before=lambda o: load(o).wait())
    high[...] = jnp.broadcast_to(jnp.max(high[...], axis=1, keepdims=True), high.shape)

    def weigh(slot, key, value, own_tile):
        v1, v2, v3 = split(value(), 3)
        gp = dot(gcat[...], jnp.concatenate([v1, v2, v1, v2, v3, v1], axis=1), NT)
        e = jnp.exp(weights[slot] - wide(high[...]))
        weights[slot] = e
        gprob[slot] = gp
        low[...] += fold(e, jnp.add)
        delta[...] += fold(e * gp, jnp.add)

    over_tiles(weigh)
    inverse = 1.0 / jnp.sum(low[...], axis=1, keepdims=True)
    low[...] = jnp.broadcast_to(inverse, low.shape)
    delta[...] = jnp.broadcast_to(jnp.sum(delta[...], axis=1, keepdims=True) * inverse, delta.shape)

    def backward(slot, key, value, own_tile):
        p = weights[slot] * wide(low[...])
        ds = p * (gprob[slot] - wide(delta[...]))
        p1, p2 = split(p, 2)
        s1, s2 = split(ds, 2)
        k1, k2 = split(key(), 2)
        kk = jnp.concatenate([k1, k2], axis=1)
        gq_acc[...] += dot(s1, kk) + dot(s2, kk)
        gkt = dot(qt[...], s1) + dot(qt[...], s2)
        gvt = dot(gt[...], p1) + dot(gt[...], p2)
        gk = (gkt[:HEAD_DIM] + gkt[HEAD_DIM:]).T
        gv = (gvt[:HEAD_DIM] + gvt[HEAD_DIM:]).T
        if own_tile == 1:
            gtail_ref[:SPAN, :] = gk
            gtail_ref[SPAN:, :] = gv
        else:
            row = branch if own_tile == 0 else slot
            gremote[row, :SPAN, :] = gk
            gremote[row, SPAN:, :] = gv

    def unseen(o):
        @pl.when((entry[o] < 0) & (o != branch))
        def _():
            gremote[o] = jnp.zeros((2 * SPAN, HEAD_DIM), jnp.float32)

    over_tiles(backward, before=unseen, after=lambda o: store(o).start())
    gq = fold(gq_acc[...], jnp.add) * logit_scale
    gq_ref[...] = jnp.concatenate([gq[:ROWS], gq[ROWS:]], axis=1)
    for o in range(BRANCHES):
        store(o).wait()


def attend(branch, fork_tile, live_len, queries, out_grad, remote, own):
    smem = pl.BlockSpec(memory_space=pltpu.SMEM)
    vmem = pl.BlockSpec(memory_space=pltpu.VMEM)
    anywhere = pl.BlockSpec(memory_space=pl.ANY)
    f32, bf16 = jnp.float32, jnp.bfloat16
    both = 2 * ROWS
    block = (2 * SPAN, HEAD_DIM)
    return pl.pallas_call(
        attend_kernel,
        out_shape=(jax.ShapeDtypeStruct((ROWS, 2 * HEAD_DIM), f32),
                   jax.ShapeDtypeStruct((BRANCHES,) + block, f32),
                   jax.ShapeDtypeStruct(block, f32)),
        in_specs=[smem] * 3 + [vmem] * 2 + [anywhere, vmem],
        out_specs=[vmem, anywhere, vmem],
        scratch_shapes=[pltpu.SMEM((BRANCHES,), jnp.int32),
                        pltpu.VMEM((BRANCHES,) + block, f32), pltpu.VMEM((BRANCHES,) + block, f32),
                        pltpu.VMEM((both, 6 * HEAD_DIM), bf16), pltpu.VMEM((both, 6 * HEAD_DIM), bf16),
                        pltpu.VMEM((2 * HEAD_DIM, both), bf16), pltpu.VMEM((2 * HEAD_DIM, both), bf16),
                        pltpu.VMEM((BRANCHES + 2, both, SPAN), f32), pltpu.VMEM((BRANCHES + 2, both, SPAN), f32),
                        pltpu.VMEM((both, HEAD_DIM), f32), pltpu.VMEM((both, HEAD_DIM), f32),
                        pltpu.VMEM((both, HEAD_DIM), f32), pltpu.VMEM((both, 2 * HEAD_DIM), f32),
                        pltpu.SemaphoreType.DMA((BRANCHES,)), pltpu.SemaphoreType.DMA((BRANCHES,))],
        compiler_params=pltpu.CompilerParams(vmem_limit_bytes=64_000_000),
    )(branch, fork_tile, live_len, queries, out_grad, remote, own)


def project_kernel(w_key_ref, w_value_ref, hidden_ref, kv_ref, remote_ref,
                   weights, hidden, left, parts, crossed, landing,
                   plane_send, plane_recv, fork_send, fork_recv, column_send, column_recv,
                   local_sem):
    depth = hidden_ref.shape[0]
    half_depth = depth // 2
    me = lax.axis_index("x") * RING + lax.axis_index("y")
    rows_in = pltpu.make_async_copy(hidden_ref, hidden, local_sem.at[0])
    rows_in.start()
    weights[me] = jnp.concatenate([w_key_ref[...], w_value_ref[...]], axis=0).T
    greet()

    def prepare():
        rows_in.wait()
        for half in (0, 1):
            h1, h2, h3 = split(hidden[half * half_depth : (half + 1) * half_depth, :].T, 3)
            left[half] = jnp.concatenate([h1, h1, h2, h2, h1, h3], axis=1)
        parts[...] = jnp.zeros_like(parts)

    def project(phase, half):
        other = turned(AXES[half][0], OFFSETS[phase - 1])
        slots = [other * RING + i if half == 0 else i * RING + other for i in range(RING)]
        rows = slice(half * half_depth, (half + 1) * half_depth)
        w1, w2, w3 = split(jnp.concatenate([weights[slot, rows, :] for slot in slots], axis=1), 3)
        product = dot(left[half], jnp.concatenate([w1, w2, w1, w2, w3, w1], axis=0))
        for i, slot in enumerate(slots):
            parts[slot] += product[:, i * HEAD_DIM : (i + 1) * HEAD_DIM]

    def both_halves(phase):
        return [functools.partial(project, phase, half) for half in (0, 1)]

    wire = Wire(plane_send, plane_recv)
    PlaneGather(wire, weights, depth).run(
        {0: [prepare], 10: both_halves(1), 12: both_halves(2), 14: both_halves(3), 15: both_halves(4)})

    column = Wire(column_send, column_recv)
    fork, tail = [
        ColumnScatter(column, 10 * i, parts, crossed.at[i], landing.at[i], i * SPAN, SPAN) for i in range(2)]
    fork.cross_begin()
    tail.cross_begin()
    fork.begin()
    fork.relay()
    fork.finish()

    def in_heads(start):
        first, second = [parts[head_slot(0, lax.axis_index("core"), q), start : start + SPAN] for q in range(2)]
        return (jnp.concatenate([first[:, :HALF], second[:, :HALF]], axis=1),
                jnp.concatenate([first[:, HALF:], second[:, HALF:]], axis=1))

    keys, values = in_heads(0)
    remote_ref[me, :SPAN] = keys
    remote_ref[me, SPAN:] = values
    kv_ref[:SPAN] = jnp.concatenate([keys, values], axis=1)
    fork_wire = Wire(fork_send, fork_recv)
    PlaneGather(fork_wire, remote_ref, 2 * SPAN).run(
        {0: [tail.begin], 5: [tail.relay], 9: [tail.finish]})
    keys, values = in_heads(SPAN)
    kv_ref[SPAN:] = jnp.concatenate([keys, values], axis=1)
    for used in (wire, column, fork_wire):
        used.drain()


def project_and_share(w_key, w_value, hidden):
    depth = hidden.shape[0]
    f32, bf16 = jnp.float32, jnp.bfloat16
    dma = pltpu.SemaphoreType.DMA
    return pl.pallas_call(
        project_kernel,
        out_shape=(jax.ShapeDtypeStruct((ROWS, 2 * HEAD_DIM), f32),
                   jax.ShapeDtypeStruct((PLANE, 2 * SPAN, HEAD_DIM), f32)),
        in_specs=[pl.BlockSpec(memory_space=pltpu.VMEM)] * 2 + [pl.BlockSpec(memory_space=pl.ANY)],
        out_specs=[pl.BlockSpec(memory_space=pltpu.VMEM)] * 2,
        scratch_shapes=[pltpu.VMEM((PLANE, depth, HEAD_DIM), f32), pltpu.VMEM((depth, ROWS), f32),
                        pltpu.VMEM((2, ROWS, 3 * depth), bf16), pltpu.VMEM((PLANE, ROWS, HEAD_DIM), f32),
                        pltpu.VMEM((2, 4, 2, SPAN, HEAD_DIM), f32), pltpu.VMEM((2, 6, SPAN, HEAD_DIM), f32),
                        dma((60,)), dma((60,)), dma((60,)), dma((60,)), dma((20,)), dma((20,)), dma((1,))],
        compiler_params=pltpu.CompilerParams(
            collective_id=1, has_side_effects=True, vmem_limit_bytes=60_000_000),
    )(w_key, w_value, hidden)


def weight_grad_kernel(remote_ref, tail_ref, hidden_ref, key_ref, value_ref, grad_ref,
                       returned, landing, grads, hidden, left, blocks, block_landing,
                       plane_send, plane_recv, block_send, block_recv, column_send, column_recv,
                       local_sem):
    depth = hidden_ref.shape[0]
    me = lax.axis_index("x") * RING + lax.axis_index("y")
    core = lax.axis_index("core")
    load = pltpu.make_async_copy(remote_ref, returned, local_sem.at[0])
    load.start()
    rows_in = pltpu.make_async_copy(hidden_ref, hidden, local_sem.at[1])
    rows_in.start()

    def place(start, keys, values):
        rows = slice(start, start + SPAN)
        for q in range(2):
            part = slice(q * HALF, (q + 1) * HALF)
            grads[head_slot(0, core, q), rows] = jnp.concatenate([keys[:, part], values[:, part]], axis=1)
        key_ref[rows] = keys
        value_ref[rows] = values

    place(SPAN, tail_ref[:SPAN], tail_ref[SPAN:])
    greet()
    load.wait()
    column = Wire(column_send, column_recv)
    fork, tail = [ColumnGather(column, 14 * i, grads, i * SPAN, SPAN) for i in range(2)]

    def prepare():
        rows_in.wait()
        for i in range(2):
            h1, h2, h3 = split(hidden[:, i * SPAN : (i + 1) * SPAN], 3)
            left[i] = jnp.concatenate([h1, h1, h2, h2, h1, h3], axis=1)

    def multiply(i, step, which):
        rows = pl.ds(i * SPAN, SPAN)
        slot = head_slot(step, which, 0)
        g1, g2, g3 = split(jnp.concatenate([grads[slot, rows, :], grads[slot + 1, rows, :]], axis=1), 3)
        product = dot(left[i], jnp.concatenate([g1, g2, g1, g2, g3, g1], axis=0))
        for q in range(2):
            new = product[:, q * HEAD_DIM : (q + 1) * HEAD_DIM]
            if i == 0:
                blocks[slot + q] += new
            else:
                blocks[slot + q] = new

    own_keys = ((12, 0, 0), (13, 0, 1))
    near_keys = ((6 + R0, 3, 0), (6 + R1, 3, 1), (6 + L0, 1, 0), (6 + L1, 1, 1))
    far_keys = ((6 + FR, 2, 0), (6 + FL, 2, 1))

    def tail_near():
        tail.near()
        multiply(1, 0, core)
        tail.partner(own_keys)
        multiply(1, 0, 1 - core)
        multiply(1, 3, core)

    def tail_far():
        tail.far()
        multiply(1, 1, core)
        tail.partner(near_keys)
        multiply(1, 3, 1 - core)

    def tail_done():
        multiply(1, 1, 1 - core)
        multiply(1, 2, core)
        tail.partner(far_keys)
        multiply(1, 2, 1 - core)

    plane = Wire(plane_send, plane_recv)
    PlaneScatter(plane, returned, landing, 2 * SPAN).run(
        {0: [tail.begin], 1: [prepare], 2: [tail.forward], 4: [tail_near], 6: [tail_far], 8: [tail_done]})
    place(0, returned[me, :SPAN], returned[me, SPAN:])
    fork.begin()

    multiply(0, 0, core)
    fork.forward()
    fork.partner(own_keys)
    multiply(0, 0, 1 - core)
    fork.near()
    multiply(0, 3, core)
    fork.far()
    multiply(0, 1, core)
    fork.partner(near_keys)
    multiply(0, 3, 1 - core)
    multiply(0, 1, 1 - core)
    multiply(0, 2, core)
    fork.partner(far_keys)
    multiply(0, 2, 1 - core)
    block_wire = Wire(block_send, block_recv)
    PlaneScatter(block_wire, blocks, block_landing, depth).run({})
    grad_ref[...] = blocks[me].T
    for used in (plane, column, block_wire):
        used.drain()


def weight_grads(grad_remote, grad_tail, hidden):
    depth = hidden.shape[0]
    f32, bf16 = jnp.float32, jnp.bfloat16
    dma = pltpu.SemaphoreType.DMA
    anywhere, vmem = pl.BlockSpec(memory_space=pl.ANY), pl.BlockSpec(memory_space=pltpu.VMEM)
    return pl.pallas_call(
        weight_grad_kernel,
        out_shape=(jax.ShapeDtypeStruct((ROWS, HEAD_DIM), f32), jax.ShapeDtypeStruct((ROWS, HEAD_DIM), f32),
                   jax.ShapeDtypeStruct((HEAD_DIM, depth), f32)),
        in_specs=[anywhere, vmem, anywhere],
        out_specs=[vmem] * 3,
        scratch_shapes=[pltpu.VMEM((PLANE, 2 * SPAN, HEAD_DIM), f32), pltpu.VMEM((60, SPAN // 2, HEAD_DIM), f32),
                        pltpu.VMEM((PLANE, ROWS, HEAD_DIM), f32), pltpu.VMEM((depth, ROWS), f32),
                        pltpu.VMEM((2, depth, 6 * SPAN), bf16), pltpu.VMEM((PLANE, depth, HEAD_DIM), f32),
                        pltpu.VMEM((60, depth // 4, HEAD_DIM), f32),
                        dma((60,)), dma((60,)), dma((60,)), dma((60,)), dma((28,)), dma((28,)),
                        dma((2,))],
        compiler_params=pltpu.CompilerParams(
            collective_id=2, has_side_effects=True, vmem_limit_bytes=60_000_000),
    )(grad_remote, grad_tail, hidden)


def results_kernel(key_in, value_in, weights_in, key_ref, value_ref, w_key_ref, w_value_ref):
    key_ref[...] = key_in[...]
    value_ref[...] = value_in[...]
    w_key_ref[...] = weights_in[:HALF]
    w_value_ref[...] = weights_in[HALF:]


def results(key, value, weights):
    f32 = jnp.float32
    vmem = pl.BlockSpec(memory_space=pltpu.VMEM)
    half = jax.ShapeDtypeStruct((HALF, weights.shape[1]), f32)
    return pl.pallas_call(
        results_kernel,
        out_shape=(jax.ShapeDtypeStruct(key.shape, f32), jax.ShapeDtypeStruct(value.shape, f32), half, half),
        in_specs=[vmem] * 3,
        out_specs=[vmem] * 4,
    )(key, value, weights)


def shards(hidden, queries, out_grad, w_key, w_value, fork_tile, live_len):
    branch = lax.axis_index(("x", "y"))[None].astype(jnp.int32)
    own, remote = project_and_share(w_key.T, w_value.T, hidden.T)
    gq, gremote, gtail = attend(branch, fork_tile, live_len, queries, out_grad, remote, own)
    key, value, gw_key, gw_value = results(*weight_grads(gremote, gtail, hidden.T))
    return gq, key, value, gw_key.T, gw_value.T


def solution(mesh):
    torus = Mesh(mesh.devices.reshape(4, 4, 4, 2), ("x", "y", "z", "core"))
    tok, head = ("x", "y"), ("z", "core")
    by_both, by_head = P(tok, head), P(head, tok)
    return jax.shard_map(
        shards,
        mesh=torus,
        in_specs=(by_both, by_both, by_both, by_head, by_head, P(), P()),
        out_specs=(by_both, by_both, by_both, by_head, by_head),
        check_vma=False,
    )
```
